256 devices in a mesh: dp: 8 (over z), section: 4 (over y_hi, core), seq: 8 (over y_lo, x).
Axes of the slice: x: 4, y: 4 (y_hi: 2, y_lo: 2; y = y_hi * 2 + y_lo), z: 8, core: 2. Of those that a mesh axis runs over, the one named last changes fastest.
Arguments:
- acts: bfloat16 [8, 1024, 1536], P('dp', 'seq'), may hold values from -6 to 6
- cotangent: bfloat16 [8, 1024, 1536], P('dp', 'seq'), may hold values from -6 to 6
- gains: bfloat16 [4, 1536], P('section'), may hold values from 0.5 to 1.5
- w_query: bfloat16 [4, 1536, 256], P('section'), may hold values from -0.15625 to 0.15625
- w_key: bfloat16 [4, 1536, 256], P('section'), may hold values from -0.15625 to 0.15625
- w_value: bfloat16 [4, 1536, 384], P('section'), may hold values from -0.15625 to 0.15625
- w_out: bfloat16 [4, 1536, 384], P('section'), may hold values from -0.3125 to 0.3125
Outputs:
- d_acts: bfloat16 [8, 1024, 1536], P('dp', 'seq', 'section')
- g_gains: float32 [4, 1536], P('section', ('dp', 'seq'))
- g_query: float32 [4, 1536, 256], P('section', ('dp', 'seq'))
- g_key: float32 [4, 1536, 256], P('section', ('dp', 'seq'))
- g_value: float32 [4, 1536, 384], P('section', ('dp', 'seq'))
- g_out: float32 [4, 1536, 384], P('section', ('dp', 'seq'))
The draws below stay inside these ranges and needn't reach their ends.
All inputs are finite; a program needn't handle non-finite values.
Results may differ from the reference program's by a relative error of at most 0.02.
Values may be sent and summed in bfloat16 or wider, within the bound.
No kernel may reach another device: no remote copies, remote signals or barrier semaphores. Data moves between devices by JAX's collectives and lax.ppermute only.
A program may use at most 64 MiB of HBM per device.

```python
import jax
import jax.numpy as jnp
from jax import lax

D = 1536
HEADS = 4
KEY = 64
VALUE = 96
SECTIONS = 4
LEN = 1024
BATCH = 8


def with_spikes(entries, rng, source, target, parts, factor):
    def block_of(dim):
        return (jnp.arange(entries.shape[dim]) // (entries.shape[dim] // parts)).reshape((-1,) + (1,) * (entries.ndim - 1 - dim))

    first = jax.random.permutation(rng, parts)[block_of(target)]
    far = (block_of(target) + parts // 2) % parts
    return jnp.where((block_of(source) == first) | (block_of(source) == far), factor * entries, entries)


def shard_levels(key, shape, shards, least, top_value):
    factor_of, own = 1.0, jax.random.fold_in(key, 6)
    for axis_at, shards_of in shards:
        heights = jnp.exp(jax.random.uniform(jax.random.fold_in(own, axis_at), (shards_of,), jnp.float32, least / len(shards), top_value / len(shards)))
        factor_of = factor_of * jnp.repeat(heights, shape[axis_at] // shards_of).reshape([-1 if axis == axis_at else 1 for axis in range(len(shape))])
    return factor_of


def bell_draw(key, extent, deviation, limit, shards=(), kind=jnp.bfloat16):
    result = deviation * jax.random.normal(key, extent, jnp.float32)
    if shards:
        result = result * shard_levels(key, extent, shards, -0.22, 0.18)
    return jnp.clip(result, -limit, limit).astype(kind)


def noise_with(key, shape, deviation, reach, split, heavy, dtype=jnp.bfloat16):
    result = deviation * jax.random.normal(key, shape, jnp.float32)
    if split:
        result = result * shard_levels(key, shape, split, -0.22, 0.18)
    return jnp.clip(with_spikes(result, jax.random.fold_in(key, 3), *heavy), -reach, reach).astype(dtype)


def setup_inputs(seed: int = 0) -> dict:
    splits = jax.random.split(jax.random.key(seed), 8)
    return {
        "acts": bell_draw(splits[0], (BATCH, LEN, D), 1.0, 6.0, ((0, 8), (1, 8))),
        "cotangent": noise_with(splits[1], (BATCH, LEN, D), 1.0, 6.0, ((0, 8), (1, 8)), (1, 2, 8, 2.0)),
        "gains": jnp.clip(1.0 + 0.1 * jax.random.normal(splits[2], (SECTIONS, D), jnp.float32), 0.5, 1.5).astype(jnp.bfloat16),
        "w_query": bell_draw(splits[3], (SECTIONS, D, HEADS * KEY), D ** -0.5, 0.15625, ((0, 4),)),
        "w_key": bell_draw(splits[4], (SECTIONS, D, HEADS * KEY), D ** -0.5, 0.15625, ((0, 4),)),
        "w_value": bell_draw(splits[5], (SECTIONS, D, HEADS * VALUE), D ** -0.5, 0.15625, ((0, 4),)),
        "w_out": bell_draw(splits[6], (SECTIONS, D, HEADS * VALUE), (HEADS * VALUE) ** -0.5, 0.3125, ((0, 4),)),
    }


epsilon = 1e-05

def layer_norm(inputs, norm_gain):
    widened = inputs.astype(jnp.float32)
    centred = widened - lax.optimization_barrier(jnp.mean(widened, axis=-1, keepdims=True))
    inverse = lax.rsqrt(lax.optimization_barrier(jnp.mean(centred * centred, axis=-1, keepdims=True)) + epsilon)
    normed = centred * inverse
    return ((normed * norm_gain.astype(jnp.float32)).astype(jnp.bfloat16), normed, inverse)

def split_heads(matrix, width):
    return matrix.astype(jnp.float32).reshape(matrix.shape[0], HEADS, width)

def exp_scores_of(query_local, key_local):
    score_scale = KEY ** (-0.5)
    return jnp.exp(jnp.einsum('ihc,jhc->hij', split_heads(query_local, KEY), split_heads(key_local, KEY)) * score_scale)

def forward_layer(inputs, weights):
    norm_gain, proj_query, proj_key, proj_value, proj_out = weights
    normal_bf, normed, inverse = layer_norm(inputs, norm_gain)
    query_local = jnp.dot(normal_bf, proj_query, preferred_element_type=jnp.float32).astype(jnp.bfloat16)
    key_local = jnp.dot(normal_bf, proj_key, preferred_element_type=jnp.float32).astype(jnp.bfloat16)
    value_local = jnp.dot(normal_bf, proj_value, preferred_element_type=jnp.float32).astype(jnp.bfloat16)
    expo = exp_scores_of(query_local, key_local)
    totals = lax.optimization_barrier(jnp.sum(expo, axis=-1))
    rounded = expo.astype(jnp.bfloat16)
    numerator = jnp.einsum('hij,jhc->ihc', rounded.astype(jnp.float32), split_heads(value_local, VALUE))
    attended = (numerator / totals.T[:, :, None]).astype(jnp.bfloat16).reshape(inputs.shape[0], HEADS * VALUE)
    mixed_out = inputs.astype(jnp.float32) + jnp.dot(attended, proj_out.T, preferred_element_type=jnp.float32)
    record = (normal_bf, normed, inverse, query_local, key_local, value_local, totals, attended)
    return (mixed_out.astype(jnp.bfloat16), record)

def backward_layer(grad_in, record, weights):
    norm_gain, proj_query, proj_key, proj_value, proj_out = weights
    normal_bf, normed, inverse, query_local, key_local, value_local, totals, attended = record
    row_count = grad_in.shape[0]
    score_scale = KEY ** (-0.5)
    grad_out_w = jnp.dot(grad_in.T, attended, preferred_element_type=jnp.float32)
    grad_attended = jnp.dot(grad_in, proj_out, preferred_element_type=jnp.float32).astype(jnp.bfloat16)
    grad_scaled = (split_heads(grad_attended, VALUE) / totals.T[:, :, None]).astype(jnp.bfloat16)
    correction = lax.optimization_barrier(jnp.sum(grad_scaled.astype(jnp.float32) * split_heads(attended, VALUE), axis=-1)).astype(jnp.bfloat16)
    expo = exp_scores_of(query_local, key_local)
    rounded = expo.astype(jnp.bfloat16)
    grad_probs = jnp.einsum('ihc,jhc->hij', grad_scaled.astype(jnp.float32), split_heads(value_local, VALUE))
    grad_scores = (expo * (grad_probs - correction.astype(jnp.float32).T[:, :, None]) * score_scale).astype(jnp.bfloat16)
    score_wide = grad_scores.astype(jnp.float32)
    grad_query = jnp.einsum('hij,jhc->ihc', score_wide, split_heads(key_local, KEY)).astype(jnp.bfloat16).reshape(row_count, HEADS * KEY)
    grad_key = jnp.einsum('hij,ihc->jhc', score_wide, split_heads(query_local, KEY)).astype(jnp.bfloat16).reshape(row_count, HEADS * KEY)
    grad_value = jnp.einsum('hij,ihc->jhc', rounded.astype(jnp.float32), grad_scaled.astype(jnp.float32)).astype(jnp.bfloat16).reshape(row_count, HEADS * VALUE)
    grad_query_w = jnp.dot(normal_bf.T, grad_query, preferred_element_type=jnp.float32)
    grad_key_w = jnp.dot(normal_bf.T, grad_key, preferred_element_type=jnp.float32)
    grad_value_w = jnp.dot(normal_bf.T, grad_value, preferred_element_type=jnp.float32)
    grad_normal = jnp.dot(grad_query, proj_query.T, preferred_element_type=jnp.float32)
    grad_normal = grad_normal + jnp.dot(grad_key, proj_key.T, preferred_element_type=jnp.float32)
    grad_normal = grad_normal + jnp.dot(grad_value, proj_value.T, preferred_element_type=jnp.float32)
    grad_gain = lax.optimization_barrier(jnp.sum(grad_normal * normed, axis=0))
    grad_normed = grad_normal * norm_gain.astype(jnp.float32)
    grad_inputs = inverse * (grad_normed - lax.optimization_barrier(jnp.mean(grad_normed, axis=-1, keepdims=True)) - normed * lax.optimization_barrier(jnp.mean(grad_normed * normed, axis=-1, keepdims=True)))
    passed = (grad_in.astype(jnp.float32) + grad_inputs).astype(jnp.bfloat16)
    return (passed, (grad_gain, grad_query_w, grad_key_w, grad_value_w, grad_out_w))

def reference(acts, cotangent, gains, w_query, w_key, w_value, w_out):

    def one_sequence(carry, pair):
        inputs, grad_flow = pair
        records = []
        for layer_index in range(SECTIONS):
            layer_weights = (gains[layer_index], w_query[layer_index], w_key[layer_index], w_value[layer_index], w_out[layer_index])
            inputs, record = forward_layer(inputs, layer_weights)
            records.append(record)
        layer_grads = [None] * SECTIONS
        for layer_index in reversed(range(SECTIONS)):
            layer_weights = (gains[layer_index], w_query[layer_index], w_key[layer_index], w_value[layer_index], w_out[layer_index])
            grad_flow, grads = backward_layer(grad_flow, records[layer_index], layer_weights)
            layer_grads[layer_index] = grads
        stacked = tuple((jnp.stack([layer_grads[layer_index][member] for layer_index in range(SECTIONS)]) for member in range(5)))
        carry = tuple((total + fresh for total, fresh in zip(carry, stacked)))
        return (carry, grad_flow)
    start_sums = (jnp.zeros((SECTIONS, D), jnp.float32), jnp.zeros((SECTIONS, D, HEADS * KEY), jnp.float32), jnp.zeros((SECTIONS, D, HEADS * KEY), jnp.float32), jnp.zeros((SECTIONS, D, HEADS * VALUE), jnp.float32), jnp.zeros((SECTIONS, D, HEADS * VALUE), jnp.float32))
    sums, d_acts = lax.scan(one_sequence, start_sums, (acts, cotangent))
    return (d_acts, sums[0], sums[1], sums[2], sums[3], sums[4])
```

```python
import functools

import jax
import jax.numpy as jnp
from jax import lax
from jax.experimental import pallas as pl
from jax.experimental.pallas import tpu as pltpu
from jax.sharding import Mesh
from jax.sharding import PartitionSpec as P

HEADS = 4
KEY = 64
VALUE = 96
QW = HEADS * KEY
VW = HEADS * VALUE
KV = QW + VW
QKV = QW + KV
ALL = QKV + VW
D = 1536
HALF = D // 2
TALL = HALF + 16
ROWS = 512
STEP = 256
MINE = 192
TERMS = ALL + 128
EPS = 1e-05
SCALE = KEY ** (-0.5)
BF = jnp.bfloat16
F32 = jnp.float32


AXES = ("dp", "yh", "core", "yl", "x")
SWAP = [(0, 1), (1, 0)]
ANY = pl.BlockSpec(memory_space=pl.ANY)
VMEM = pl.BlockSpec(memory_space=pltpu.VMEM)
SMEM = pl.BlockSpec(memory_space=pltpu.SMEM)


def dot(a, b):
    return lax.dot_general(a, b, (((1,), (0,)), ((), ())), preferred_element_type=F32)


def dot_t(a, b):
    return lax.dot_general(a, b, (((1,), (1,)), ((), ())), preferred_element_type=F32)


def lanes(width):
    return lax.broadcasted_iota(jnp.int32, (1, width), 1)


WINDOWS = ((0, 128), (0, 256), (128, 384), (256, 384))


def fetch(refs, layer, where, first, last, dst, sems):
    near = layer < 2
    on_own = where[0] == layer % 2

    def start(pair):
        for k in range(2):
            if near:
                src, slot = pair.at[k], k
            else:
                src = pair[k]
                slot = where[1] if k == 0 else 1 - where[1]
            pltpu.make_async_copy(
                src.at[:, pl.ds(first, last - first)], dst.at[slot], sems.at[k]
            ).start()

    own, other = (refs[0], refs[1]) if near else (refs[:2], refs[2:])
    pl.when(on_own)(lambda: start(own))
    pl.when(jnp.logical_not(on_own))(lambda: start(other))


def fetched(dst, sems):
    for k in range(2):
        pltpu.make_async_copy(dst.at[k], dst.at[k], sems.at[k]).wait()


def gain_row(w):
    rest = D - ALL
    return jnp.concatenate(
        [w[0, HALF : HALF + 1, :].astype(F32), w[0, HALF + 1 : HALF + 2, :rest].astype(F32)], 1
    )


def norm(x):
    wide = x.astype(F32)
    centred = wide - jnp.mean(wide, axis=-1, keepdims=True)
    inverse = lax.rsqrt(jnp.mean(centred * centred, axis=-1, keepdims=True) + EPS)
    return centred * inverse, inverse


def project(x, gain, w):
    normed, _ = norm(x)
    normal = (normed * gain).astype(BF)
    out = dot(normal[:, :HALF], w[0, :HALF, :QKV]) + dot(normal[:, HALF:], w[1, :HALF, :QKV])
    return out.astype(BF)


def head_query(q, h):
    mask = jnp.where(lanes(128) // KEY == h % 2, SCALE, 0.0).astype(BF)
    g = h // 2
    return q[:, 128 * g : 128 * g + 128] * mask


def first_kernel(layer, where, x_ref, *rest):
    count = 2 if layer < 2 else 4
    refs, (qkv_ref, w, sems) = rest[:count], rest[count:]
    fetch(refs, layer, where, 0, ALL, w, sems)
    fetched(w, sems)
    gain = gain_row(w)
    for i in range(ROWS // STEP):
        rows = pl.ds(i * STEP, STEP)
        qkv_ref[rows, :] = project(x_ref[rows, :], gain, w)


def forward_kernel(layer, where, qkv_ref, kv_ref, x_ref, *rest):
    counts = [2 if layer < 2 else 4, 2 if layer + 1 < 2 else 4]
    refs_out, rest = rest[: counts[0]], rest[counts[0] :]
    refs_next, rest = rest[: counts[1]], rest[counts[1] :]
    att_ref, tot_ref, out_ref, next_ref, wo, w, sems = rest
    fetch(refs_out, layer, where, QKV, ALL, wo, sems.at[0])
    fetch(refs_next, layer + 1, where, 0, ALL, w, sems.at[1])

    def attend(i, carry):
        attention_step(pl.ds(pl.multiple_of(i * STEP, STEP), STEP), qkv_ref, kv_ref, att_ref, tot_ref)
        return carry

    lax.fori_loop(0, ROWS // STEP, attend, 0)
    fetched(wo, sems.at[0])
    fetched(w, sems.at[1])
    gain = gain_row(w)

    def finish(i, carry):
        rows = pl.ds(pl.multiple_of(i * STEP, STEP), STEP)
        attended = att_ref[rows, :]
        mixed = jnp.concatenate(
            [dot_t(attended, wo[0, :HALF, :]), dot_t(attended, wo[1, :HALF, :])], 1
        )
        out = (x_ref[rows, :].astype(F32) + mixed).astype(BF)
        out_ref[rows, :] = out
        next_ref[rows, :] = project(out, gain, w)
        return carry

    lax.fori_loop(0, ROWS // STEP, finish, 0)


def last_kernel(qkv_ref, kv_ref, att_ref, tot_ref):
    def attend(i, carry):
        attention_step(pl.ds(pl.multiple_of(i * STEP, STEP), STEP), qkv_ref, kv_ref, att_ref, tot_ref)
        return carry

    lax.fori_loop(0, ROWS // STEP, attend, 0)


def attention_step(rows, qkv_ref, kv_ref, att_ref, tot_ref):
    q = qkv_ref[rows, :QW]
    attended = jnp.zeros((STEP, VW), F32)
    channel = lanes(VW) // VALUE
    for h in range(HEADS):
        g = 128 * (h // 2)
        qh = head_query(q, h)
        e_own = jnp.exp(dot_t(qh, qkv_ref[:, QW + g : QW + g + 128]))
        e_far = jnp.exp(dot_t(qh, kv_ref[:, g : g + 128]))
        total = jnp.sum(e_own + e_far, axis=-1, keepdims=True)
        lo, hi = WINDOWS[h]
        num = dot(e_own.astype(BF), qkv_ref[:, 2 * QW + lo : 2 * QW + hi]) + dot(
            e_far.astype(BF), kv_ref[:, QW + lo : QW + hi]
        )
        part = num / total
        pieces = []
        if lo:
            pieces.append(jnp.zeros((STEP, lo), F32))
        pieces.append(part)
        if hi < VW:
            pieces.append(jnp.zeros((STEP, VW - hi), F32))
        wide = jnp.concatenate(pieces, 1) if len(pieces) > 1 else part
        attended = jnp.where(channel == h, wide, attended)
        tot_ref[rows, h : h + 1] = total
    att_ref[rows, :] = attended.astype(BF)


def scores_kernel(layer, where, grad_ref, qkv_ref, kv_ref, att_ref, tot_ref, *rest):
    count = 2 if layer < 2 else 4
    refs, (gq_ref, own_ref, far_ref, acc, wo, sems) = rest[:count], rest[count:]
    fetch(refs, layer, where, QKV, ALL, wo, sems)
    acc[...] = jnp.zeros_like(acc)
    fetched(wo, sems)
    channel = lanes(VW) // VALUE
    key_lane = lanes(128) // KEY

    def step(i, carry):
        rows = pl.ds(pl.multiple_of(i * STEP, STEP), STEP)
        grad = grad_ref[rows, :]
        g_att = (
            dot(grad[:, :HALF], wo[0, :HALF, :]) + dot(grad[:, HALF:], wo[1, :HALF, :])
        ).astype(BF)
        tot = tot_ref[rows, :]
        divisor = jnp.ones((STEP, VW), F32)
        for h in range(HEADS):
            divisor = jnp.where(channel == h, tot[:, h : h + 1], divisor)
        scaled_wide = (g_att.astype(F32) / divisor).astype(BF).astype(F32)
        scaled = scaled_wide.astype(BF)
        products = scaled_wide * att_ref[rows, :].astype(F32)
        scaled_t = scaled_wide.T.astype(BF)
        q = qkv_ref[rows, :QW]
        q_t = q.astype(F32).T.astype(BF)
        gq = [None, None]
        for h in range(HEADS):
            g = 128 * (h // 2)
            lo, hi = WINDOWS[h]
            corr = jnp.sum(jnp.where(channel == h, products, 0.0), axis=-1, keepdims=True)
            corr = corr.astype(BF).astype(F32)
            qh = head_query(q, h)
            sh = jnp.where(channel == h, scaled, jnp.zeros_like(scaled))[:, lo:hi]
            got = None
            for side in range(2):
                if side == 0:
                    k = qkv_ref[:, QW + g : QW + g + 128]
                    v = qkv_ref[:, 2 * QW + lo : 2 * QW + hi]
                else:
                    k = kv_ref[:, g : g + 128]
                    v = kv_ref[:, QW + lo : QW + hi]
                e = jnp.exp(dot_t(qh, k))
                gp = dot_t(sh, v)
                sg = (e * (gp - corr) * SCALE).astype(BF)
                more = dot(sg, k)
                got = more if got is None else got + more
                at = pl.ds(side * ROWS, ROWS)
                acc[KEY * h : KEY * h + KEY, at] += dot(q_t[KEY * h : KEY * h + KEY, :], sg)
                acc[QW + VALUE * h : QW + VALUE * h + VALUE, at] += dot(
                    scaled_t[VALUE * h : VALUE * h + VALUE, :], e.astype(BF)
                )
            p = h // 2
            gq[p] = got if h % 2 == 0 else jnp.where(key_lane == 1, got, gq[p])
        gq_ref[rows, :] = jnp.concatenate(gq, 1).astype(BF)
        return carry

    lax.fori_loop(0, ROWS // STEP, step, 0)
    own_ref[...] = acc[:, :ROWS]
    far_ref[...] = acc[:, ROWS:].astype(BF)


def inputs_kernel(layer, where, own_ref, got_ref, gq_ref, x_ref, grad_ref, att_ref, pick_ref, *rest):
    count = 2 if layer < 2 else 4
    refs, (pass_ref, term_ref, gqkv, normal, gg, w, sems) = rest[:count], rest[count:]
    fetch(refs, layer, where, 0, ALL, w, sems)
    gqkv[:, QW:] = (own_ref[...] + got_ref[...].astype(F32)).T.astype(BF)
    gqkv[:, :QW] = gq_ref[...]
    gg[...] = jnp.zeros_like(gg)
    fetched(w, sems)
    gain = gain_row(w)

    def step(i, carry):
        rows = pl.ds(pl.multiple_of(i * STEP, STEP), STEP)
        g = gqkv[rows, :]
        g_normal = jnp.concatenate(
            [dot_t(g, w[0, :HALF, :QKV]), dot_t(g, w[1, :HALF, :QKV])], 1
        )
        normed, inverse = norm(x_ref[rows, :])
        normal[rows, :] = (normed * gain).astype(BF)
        gg[...] += jnp.sum(g_normal * normed, axis=0, keepdims=True)
        g_normed = g_normal * gain
        g_x = inverse * (
            g_normed
            - jnp.mean(g_normed, axis=-1, keepdims=True)
            - normed * jnp.mean(g_normed * normed, axis=-1, keepdims=True)
        )
        pass_ref[rows, :] = (grad_ref[rows, :].astype(F32) + g_x).astype(BF)
        return carry

    lax.fori_loop(0, ROWS // STEP, step, 0)
    pick = pick_ref[...]
    term_ref[:, :QKV] = dot(dot_t(pick, normal[...]).astype(BF), gqkv[...])
    term_ref[:, QKV:ALL] = dot(dot_t(pick, grad_ref[...]).astype(BF), att_ref[...])
    total = gg[...]
    high = total.astype(BF)
    low = (total - high.astype(F32)).astype(BF)
    both = jnp.concatenate(
        [jnp.broadcast_to(high, (64, D)), jnp.broadcast_to(low, (64, D))], 0
    )
    picked = dot_t(pick, both)
    term_ref[:, ALL:] = picked + pltpu.roll(picked, 64, 1)


def shape(*dims, dtype=BF):
    return jax.ShapeDtypeStruct(dims, dtype)


def call(kernel, out_shape, in_specs, scratch, name, limit=40):
    outs = jax.tree.map(lambda _: VMEM, out_shape)
    return pl.pallas_call(
        kernel,
        out_shape=out_shape,
        in_specs=in_specs,
        out_specs=outs,
        scratch_shapes=scratch,
        name=name,
        compiler_params=pltpu.CompilerParams(vmem_limit_bytes=limit << 20),
    )


W_ALL = pltpu.VMEM((2, TALL, ALL), BF)
W_OUT = pltpu.VMEM((2, TALL, VW), BF)
SEMS = pltpu.SemaphoreType.DMA((2,))


def first(layer, where, x, ws):
    return call(
        functools.partial(first_kernel, layer),
        shape(ROWS, QKV),
        [SMEM, VMEM] + [ANY] * len(ws),
        [W_ALL, SEMS],
        "first",
    )(where, x, *ws)


def forward(layer, where, qkv, kv, x, ws, ws_next):
    return call(
        functools.partial(forward_kernel, layer),
        (shape(ROWS, VW), shape(ROWS, 128, dtype=F32), shape(ROWS, D), shape(ROWS, QKV)),
        [SMEM, VMEM, VMEM, VMEM] + [ANY] * (len(ws) + len(ws_next)),
        [W_OUT, W_ALL, pltpu.SemaphoreType.DMA((2, 2))],
        f"forward{layer}",
    )(where, qkv, kv, x, *ws, *ws_next)


def last(qkv, kv):
    return call(
        last_kernel,
        (shape(ROWS, VW), shape(ROWS, 128, dtype=F32)),
        [VMEM, VMEM],
        [],
        "forward3",
    )(qkv, kv)


def score_grads(layer, where, grad, qkv, kv, att, tot, ws):
    return call(
        functools.partial(scores_kernel, layer),
        (shape(ROWS, QW), shape(KV, ROWS, dtype=F32), shape(KV, ROWS)),
        [SMEM] + [VMEM] * 5 + [ANY] * len(ws),
        [pltpu.VMEM((KV, 2 * ROWS), F32), W_OUT, SEMS],
        f"scores{layer}",
    )(where, grad, qkv, kv, att, tot, *ws)


def input_grads(layer, where, own, got, gq, x, grad, att, pick, ws):
    return call(
        functools.partial(inputs_kernel, layer),
        (shape(ROWS, D), shape(MINE, TERMS, dtype=F32)),
        [SMEM] + [VMEM] * 7 + [ANY] * len(ws),
        [
            pltpu.VMEM((ROWS, QKV), BF),
            pltpu.VMEM((ROWS, D), BF),
            pltpu.VMEM((1, D), F32),
            W_ALL,
            SEMS,
        ],
        f"inputs{layer}",
    )(where, own, got, gq, x, grad, att, pick, *ws)


def after(value, *deps):
    return lax.optimization_barrier((value, *deps))[0]


def gather_rows(block):
    block = lax.ppermute(block, ("core", "yl"), [(0, 0), (1, 2), (2, 1), (3, 3)])
    me = lax.axis_index("x")
    parts = [block] + [
        lax.ppermute(block, "x", [(i, (i + k) % 4) for i in range(4)]) for k in (1, 2, 3)
    ]
    rows = jnp.zeros((4,) + block.shape, block.dtype)
    for k in range(4):
        rows = lax.dynamic_update_index_in_dim(rows, parts[k], (me - k) % 4, 0)
    return rows.reshape(4 * block.shape[0], block.shape[1])


def shards(acts, cotangent, gains, w_query, w_key, w_value, w_out):
    core = lax.axis_index("core")
    yh = lax.axis_index("yh")
    yl = lax.axis_index("yl")
    lane = lax.axis_index("x")
    odd = lax.axis_index("dp") % 2
    spot = yl * 4 + lane
    where = jnp.stack([core, odd]).astype(jnp.int32)

    matrices = jnp.concatenate([w_query[0], w_key[0], w_value[0], w_out[0]], 1)
    matrices = matrices.reshape(2, HALF, ALL)
    gain_rows = jnp.pad(gains[0], (0, 16 * ALL - D)).reshape(1, 16, ALL)
    own = jnp.concatenate([matrices, jnp.concatenate([gain_rows, gain_rows], 0)], 1)

    x = gather_rows(acts[0])
    other = lax.ppermute(own, "core", SWAP)
    mine = lax.dynamic_index_in_dim(own, odd, 0, False)

    def fetch_far(half, sender):
        half = lax.ppermute(half, ("yh", "core"), [(2 + sender, sender)])
        return half

    def spread(half, sender):
        theirs = lax.ppermute(half, "dp", [(i, i ^ 1) for i in range(8)])
        half_2 = lax.ppermute(half, "core", [(sender, 1 - sender)])
        theirs_2 = lax.ppermute(theirs, "core", [(sender, 1 - sender)])
        return (half, theirs, half_2, theirs_2)

    far_2 = fetch_far(mine, 0)
    far_3 = fetch_far(after(mine, far_2), 1)
    weights = [(own, other), (own, other), spread(far_2, 0), spread(far_3, 1)]
    grad = gather_rows(after(cotangent[0], x))

    column = jnp.arange(D)
    wanted = (jnp.arange(MINE) // 24) * MINE + spot * 24 + jnp.arange(MINE) % 24
    pick = (column[None, :] == wanted[:, None]).astype(BF)

    saved = []
    qkv = first(0, where, x, weights[0])
    for layer in range(4):
        kv = lax.ppermute(qkv[:, QW:], "core", SWAP)
        if layer < 3:
            att, tot, out, after_qkv = forward(
                layer, where, qkv, kv, x, weights[layer], weights[layer + 1]
            )
        else:
            att, tot = last(qkv, kv)
            out = after_qkv = None
        saved.append((x, qkv, kv, att, tot))
        x, qkv = out, after_qkv

    def meet(first_terms, second_terms):
        keep = jnp.where(core == 0, first_terms, second_terms)
        send = jnp.where(core == 0, second_terms, first_terms)
        return (keep + lax.ppermute(send, "core", SWAP)).astype(BF)

    terms = [None] * 4
    far = None
    for layer in (3, 2, 1, 0):
        x, qkv, kv, att, tot = saved[layer]
        gq, own_part, far_part = score_grads(
            layer, where, grad, qkv, kv, att, tot, weights[layer]
        )
        got = lax.ppermute(far_part, "core", SWAP)
        grad, terms[layer] = input_grads(
            layer, where, own_part, got, gq, x, grad, att, pick, weights[layer]
        )
        if layer == 2:
            far = lax.ppermute(meet(terms[2], terms[3]), "yh", [(0, 1)])

    block = lax.dynamic_slice_in_dim(grad, lane * 128, 128, 0)
    even_part = jnp.concatenate([block[:, :384], block[:, 768:1152]], 1)
    odd_part = jnp.concatenate([block[:, 384:768], block[:, 1152:]], 1)
    to_other = jnp.where(core == 0, odd_part, even_part)
    kept = jnp.where(core == 0, even_part, odd_part)
    both = jnp.where(core == yl, kept, lax.ppermute(to_other, "core", SWAP))
    d_far = lax.ppermute(both[:, 384:], "yh", [(0, 1)])
    d_acts = jnp.where(yh == 0, both[:, :384], d_far)

    near = meet(terms[0], terms[1])
    payload = jnp.where(yh == 0, near, far).reshape(8, 24, TERMS)
    sums = jnp.sum(lax.all_to_all(payload, "dp", 0, 0).astype(F32), axis=0)
    return (
        d_acts[None],
        sums[:, ALL].reshape(1, 24),
        sums[None, :, :QW],
        sums[None, :, QW : 2 * QW],
        sums[None, :, 2 * QW : QKV],
        sums[None, :, QKV:ALL],
    )


def solution(mesh):
    fine = Mesh(mesh.devices.reshape(8, 2, 2, 2, 4), AXES)
    section = ("yh", "core")
    seq = ("yl", "x")
    rows = ("dp", "yl", "x")
    return jax.shard_map(
        shards,
        mesh=fine,
        in_specs=(
            P("dp", seq, None),
            P("dp", seq, None),
            P(section, None),
            P(section, None, None),
            P(section, None, None),
            P(section, None, None),
            P(section, None, None),
        ),
        out_specs=(
            P("dp", seq, section),
            P(section, rows),
            P(section, rows, None),
            P(section, rows, None),
            P(section, rows, None),
            P(section, rows, None),
        ),
        check_vma=False,
    )
```

```python
import functools

import jax
import jax.numpy as jnp
from jax import lax
from jax.experimental import pallas as pl
from jax.experimental.pallas import tpu as pltpu
from jax.sharding import Mesh
from jax.sharding import PartitionSpec as P

HEADS = 4
KEY = 64
VALUE = 96
QW = HEADS * KEY
VW = HEADS * VALUE
KV = QW + VW
QKV = QW + KV
ALL = QKV + VW
D = 1536
UNIT = 208
TALL = 8 * UNIT
ROWS = 512
STEP = 256
MINE = 192
TERMS = ALL + 128
EPS = 1e-05
SCALE = KEY ** (-0.5)
BF = jnp.bfloat16
F32 = jnp.float32


AXES = ("dp", "yh", "core", "yl", "x")
SWAP = [(0, 1), (1, 0)]
ANY = pl.BlockSpec(memory_space=pl.ANY)
VMEM = pl.BlockSpec(memory_space=pltpu.VMEM)
SMEM = pl.BlockSpec(memory_space=pltpu.SMEM)


def dot(a, b):
    return lax.dot_general(a, b, (((1,), (0,)), ((), ())), preferred_element_type=F32)


def dot_t(a, b):
    return lax.dot_general(a, b, (((1,), (1,)), ((), ())), preferred_element_type=F32)


def lanes(width):
    return lax.broadcasted_iota(jnp.int32, (1, width), 1)


WINDOWS = ((0, 128), (0, 256), (128, 384), (256, 384))


def fetch(refs, layer, where, first, last, dst, sems):
    span = pl.ds(first, last - first)
    if layer < 2:
        on_own = where[0] == layer % 2
        own = pltpu.make_async_copy(refs[0].at[:, span], dst, sems.at[0])
        other = pltpu.make_async_copy(refs[1].at[:, span], dst, sems.at[0])
        pl.when(on_own)(own.start)
        pl.when(jnp.logical_not(on_own))(other.start)
        return own.wait
    core, odd = where[0], where[1]
    copies = []
    for k in range(2):
        near = 4 * odd + 2 * jnp.bitwise_xor(core, k)
        away = 4 * (1 - odd) + 2 * jnp.bitwise_xor(core, k)
        for j, (unit, count) in enumerate(((near, 2), (away, 1), (away + 1, 1))):
            start = pl.multiple_of(unit * UNIT, 16)
            copy = pltpu.make_async_copy(
                refs[3 * k + j].at[:, span],
                dst.at[pl.ds(start, count * UNIT)],
                sems.at[3 * k + j],
            )
            copy.start()
            copies.append(copy)
    return lambda: [copy.wait() for copy in copies]


def gain_row(w):
    return jnp.concatenate(
        [w[D : D + 1, :].astype(F32), w[D + 1 : D + 2, : D - QKV].astype(F32)], 1
    )


def norm(x):
    wide = x.astype(F32)
    centred = wide - jnp.mean(wide, axis=-1, keepdims=True)
    inverse = lax.rsqrt(jnp.mean(centred * centred, axis=-1, keepdims=True) + EPS)
    return centred * inverse, inverse


def project(x, gain, w):
    normed, _ = norm(x)
    return dot((normed * gain).astype(BF), w[:D, :]).astype(BF)


def head_query(q, h):
    mask = jnp.where(lanes(128) // KEY == h % 2, SCALE, 0.0).astype(BF)
    g = h // 2
    return q[:, 128 * g : 128 * g + 128] * mask


def project_kernel(layer, where, x_ref, *rest):
    refs, (qkv_ref, w, sems) = rest[:-3], rest[-3:]
    fetch(refs, layer, where, 0, QKV, w, sems)()
    gain = gain_row(w)

    def step(i, carry):
        rows = pl.ds(pl.multiple_of(i * STEP, STEP), STEP)
        qkv_ref[rows, :] = project(x_ref[rows, :], gain, w)
        return carry

    lax.fori_loop(0, ROWS // STEP, step, 0)


def attend_kernel(layer, where, qkv_ref, kv_ref, x_ref, *rest):
    count = 2 if layer < 2 else 6
    refs, rest = rest[:count], rest[count:]
    if layer == 0:
        att_ref, tot_ref, out_ref, next_ref, wo, sems, w, sems_w = rest[-8:]
        ready_w = fetch(refs, 1, where, 0, QKV, w, sems_w)
    else:
        att_ref, tot_ref, out_ref, wo, sems = rest
    ready = fetch(refs, layer, where, QKV, ALL, wo, sems)

    def attend(i, carry):
        rows = pl.ds(pl.multiple_of(i * STEP, STEP), STEP)
        attention_step(rows, qkv_ref, kv_ref, att_ref, tot_ref)
        return carry

    lax.fori_loop(0, ROWS // STEP, attend, 0)
    ready()
    if layer == 0:
        ready_w()
        gain = gain_row(w)

    def finish(i, carry):
        rows = pl.ds(pl.multiple_of(i * STEP, STEP), STEP)
        mixed = dot_t(att_ref[rows, :], wo[:D, :])
        out = (x_ref[rows, :].astype(F32) + mixed).astype(BF)
        out_ref[rows, :] = out
        if layer == 0:
            next_ref[rows, :] = project(out, gain, w)
        return carry

    lax.fori_loop(0, ROWS // STEP, finish, 0)


def last_kernel(qkv_ref, kv_ref, att_ref, tot_ref):
    def attend(i, carry):
        attention_step(pl.ds(pl.multiple_of(i * STEP, STEP), STEP), qkv_ref, kv_ref, att_ref, tot_ref)
        return carry

    lax.fori_loop(0, ROWS // STEP, attend, 0)


def attention_step(rows, qkv_ref, kv_ref, att_ref, tot_ref):
    q = qkv_ref[rows, :QW]
    attended = jnp.zeros((STEP, VW), F32)
    channel = lanes(VW) // VALUE
    for h in range(HEADS):
        g = 128 * (h // 2)
        qh = head_query(q, h)
        e_own = jnp.exp(dot_t(qh, qkv_ref[:, QW + g : QW + g + 128]))
        e_far = jnp.exp(dot_t(qh, kv_ref[:, g : g + 128]))
        total = jnp.sum(e_own + e_far, axis=-1, keepdims=True)
        lo, hi = WINDOWS[h]
        num = dot(e_own.astype(BF), qkv_ref[:, 2 * QW + lo : 2 * QW + hi]) + dot(
            e_far.astype(BF), kv_ref[:, QW + lo : QW + hi]
        )
        part = num / total
        pieces = []
        if lo:
            pieces.append(jnp.zeros((STEP, lo), F32))
        pieces.append(part)
        if hi < VW:
            pieces.append(jnp.zeros((STEP, VW - hi), F32))
        wide = jnp.concatenate(pieces, 1) if len(pieces) > 1 else part
        attended = jnp.where(channel == h, wide, attended)
        tot_ref[rows, h : h + 1] = total
    att_ref[rows, :] = attended.astype(BF)


def scores_kernel(layer, where, grad_ref, qkv_ref, kv_ref, att_ref, tot_ref, *rest):
    refs, (gq_ref, own_ref, far_ref, acc, wo, sems) = rest[:-6], rest[-6:]
    ready = fetch(refs, layer, where, QKV, ALL, wo, sems)
    acc[...] = jnp.zeros_like(acc)
    ready()
    channel = lanes(VW) // VALUE
    key_lane = lanes(128) // KEY

    def step(i, carry):
        rows = pl.ds(pl.multiple_of(i * STEP, STEP), STEP)
        grad = grad_ref[rows, :]
        g_att = dot(grad, wo[:D, :]).astype(BF)
        tot = tot_ref[rows, :]
        divisor = jnp.ones((STEP, VW), F32)
        for h in range(HEADS):
            divisor = jnp.where(channel == h, tot[:, h : h + 1], divisor)
        scaled_wide = (g_att.astype(F32) / divisor).astype(BF).astype(F32)
        scaled = scaled_wide.astype(BF)
        products = scaled_wide * att_ref[rows, :].astype(F32)
        scaled_t = scaled_wide.T.astype(BF)
        q = qkv_ref[rows, :QW]
        q_t = q.astype(F32).T.astype(BF)
        gq = [None, None]
        for h in range(HEADS):
            g = 128 * (h // 2)
            lo, hi = WINDOWS[h]
            corr = jnp.sum(jnp.where(channel == h, products, 0.0), axis=-1, keepdims=True)
            corr = corr.astype(BF).astype(F32)
            qh = head_query(q, h)
            sh = jnp.where(channel == h, scaled, jnp.zeros_like(scaled))[:, lo:hi]
            got = None
            for side in range(2):
                if side == 0:
                    k = qkv_ref[:, QW + g : QW + g + 128]
                    v = qkv_ref[:, 2 * QW + lo : 2 * QW + hi]
                else:
                    k = kv_ref[:, g : g + 128]
                    v = kv_ref[:, QW + lo : QW + hi]
                e = jnp.exp(dot_t(qh, k))
                gp = dot_t(sh, v)
                sg = (e * (gp - corr) * SCALE).astype(BF)
                more = dot(sg, k)
                got = more if got is None else got + more
                at = pl.ds(side * ROWS, ROWS)
                acc[KEY * h : KEY * h + KEY, at] += dot(q_t[KEY * h : KEY * h + KEY, :], sg)
                acc[QW + VALUE * h : QW + VALUE * h + VALUE, at] += dot(
                    scaled_t[VALUE * h : VALUE * h + VALUE, :], e.astype(BF)
                )
            p = h // 2
            gq[p] = got if h % 2 == 0 else jnp.where(key_lane == 1, got, gq[p])
        gq_ref[rows, :] = jnp.concatenate(gq, 1).astype(BF)
        return carry

    lax.fori_loop(0, ROWS // STEP, step, 0)
    own_ref[...] = acc[:, :ROWS]
    far_ref[...] = acc[:, ROWS:].astype(BF)


def inputs_kernel(layer, where, own_ref, got_ref, gq_ref, x_ref, grad_ref, att_ref, pick_ref, *rest):
    refs, (pass_ref, term_ref, gqkv, normal, gg, w, sems) = rest[:-7], rest[-7:]
    ready = fetch(refs, layer, where, 0, QKV, w, sems)
    gqkv[:, QW:] = (own_ref[...] + got_ref[...].astype(F32)).T.astype(BF)
    gqkv[:, :QW] = gq_ref[...]
    gg[...] = jnp.zeros_like(gg)
    ready()
    gain = gain_row(w)

    def step(i, carry):
        rows = pl.ds(pl.multiple_of(i * STEP, STEP), STEP)
        g = gqkv[rows, :]
        g_normal = dot_t(g, w[:D, :])
        normed, inverse = norm(x_ref[rows, :])
        normal[rows, :] = (normed * gain).astype(BF)
        gg[...] += jnp.sum(g_normal * normed, axis=0, keepdims=True)
        g_normed = g_normal * gain
        g_x = inverse * (
            g_normed
            - jnp.mean(g_normed, axis=-1, keepdims=True)
            - normed * jnp.mean(g_normed * normed, axis=-1, keepdims=True)
        )
        pass_ref[rows, :] = (grad_ref[rows, :].astype(F32) + g_x).astype(BF)
        return carry

    lax.fori_loop(0, ROWS // STEP, step, 0)
    pick = pick_ref[...]
    term_ref[:, :QKV] = dot(dot_t(pick, normal[...]).astype(BF), gqkv[...])
    term_ref[:, QKV:ALL] = dot(dot_t(pick, grad_ref[...]).astype(BF), att_ref[...])
    total = gg[...]
    high = total.astype(BF)
    low = (total - high.astype(F32)).astype(BF)
    both = jnp.concatenate(
        [jnp.broadcast_to(high, (64, D)), jnp.broadcast_to(low, (64, D))], 0
    )
    picked = dot_t(pick, both)
    term_ref[:, ALL:] = picked + pltpu.roll(picked, 64, 1)


def shape(*dims, dtype=BF):
    return jax.ShapeDtypeStruct(dims, dtype)


def call(kernel, out_shape, in_specs, scratch, limit=40):
    outs = jax.tree.map(lambda _: VMEM, out_shape)
    return pl.pallas_call(
        kernel,
        out_shape=out_shape,
        in_specs=in_specs,
        out_specs=outs,
        scratch_shapes=scratch,
        compiler_params=pltpu.CompilerParams(vmem_limit_bytes=limit << 20),
    )


W_IN = pltpu.VMEM((TALL, QKV), BF)
W_OUT = pltpu.VMEM((TALL, VW), BF)
SEMS = pltpu.SemaphoreType.DMA((6,))


def first(layer, where, x, ws):
    return call(
        functools.partial(project_kernel, layer),
        shape(ROWS, QKV),
        [SMEM, VMEM] + [ANY] * len(ws),
        [W_IN, SEMS],
    )(where, x, *ws)


def attend(layer, where, qkv, kv, x, ws):
    out_shape = [shape(ROWS, VW), shape(ROWS, 128, dtype=F32), shape(ROWS, D)]
    scratch = [W_OUT, SEMS]
    if layer == 0:
        out_shape.append(shape(ROWS, QKV))
        scratch += [W_IN, SEMS]
    return call(
        functools.partial(attend_kernel, layer),
        out_shape,
        [SMEM, VMEM, VMEM, VMEM] + [ANY] * len(ws),
        scratch,
    )(where, qkv, kv, x, *ws)


def last(qkv, kv):
    return call(
        last_kernel, (shape(ROWS, VW), shape(ROWS, 128, dtype=F32)), [VMEM, VMEM], []
    )(qkv, kv)


def score_grads(layer, where, grad, qkv, kv, att, tot, ws):
    return call(
        functools.partial(scores_kernel, layer),
        (shape(ROWS, QW), shape(KV, ROWS, dtype=F32), shape(KV, ROWS)),
        [SMEM] + [VMEM] * 5 + [ANY] * len(ws),
        [pltpu.VMEM((KV, 2 * ROWS), F32), W_OUT, SEMS],
    )(where, grad, qkv, kv, att, tot, *ws)


def input_grads(layer, where, own, got, gq, x, grad, att, pick, ws):
    return call(
        functools.partial(inputs_kernel, layer),
        (shape(ROWS, D), shape(MINE, TERMS, dtype=F32)),
        [SMEM] + [VMEM] * 7 + [ANY] * len(ws),
        [
            pltpu.VMEM((ROWS, QKV), BF),
            pltpu.VMEM((ROWS, D), BF),
            pltpu.VMEM((1, D), F32),
            W_IN,
            SEMS,
        ],
    )(where, own, got, gq, x, grad, att, pick, *ws)


def after(value, *deps):
    return lax.optimization_barrier((value, *deps))[0]


def ring(count, k):
    return [(i, (i + k) % count) for i in range(count)]


def swapped(block):
    return lax.ppermute(block, ("core", "yl"), [(0, 0), (1, 2), (2, 1), (3, 3)])


def gather_rows(block):
    me = lax.axis_index("x")
    parts = [block] + [lax.ppermute(block, "x", ring(4, k)) for k in (1, 2, 3)]
    rows = jnp.zeros((4,) + block.shape, block.dtype)
    for k in range(4):
        rows = lax.dynamic_update_index_in_dim(rows, parts[k], (me - k) % 4, 0)
    return rows.reshape(4 * block.shape[0], block.shape[1])


def packed(gains, w_query, w_key, w_value, w_out):
    gain_rows = jnp.concatenate([gains[0], jnp.zeros(2 * QKV - D, BF)]).reshape(2, QKV)
    gain_rows = jnp.pad(gain_rows, ((0, TALL - D - 2), (0, ALL - QKV)))
    matrices = jnp.concatenate([w_query[0], w_key[0], w_value[0], w_out[0]], 1)
    return jnp.concatenate([matrices, gain_rows], 0)


def program(acts, cotangent, gains, w_query, w_key, w_value, w_out):
    core = lax.axis_index("core")
    yh = lax.axis_index("yh")
    yl = lax.axis_index("yl")
    lane = lax.axis_index("x")
    odd = lax.axis_index("dp") % 2
    spot = yl * 4 + lane
    where = jnp.stack([core, odd]).astype(jnp.int32)

    block = swapped(acts[0])
    own = packed(gains, w_query, w_key, w_value, w_out)
    other = lax.ppermute(own, "core", SWAP)
    x = gather_rows(block)

    quarter = 4 * odd + 2 * core

    def fetch_far(layer):
        near = lax.dynamic_slice_in_dim(own, quarter * UNIT, 2 * UNIT, 0)
        away = lax.dynamic_slice_in_dim(other, quarter * UNIT, 2 * UNIT, 0)
        piece = jnp.where(core == layer % 2, near, away)
        return piece

    def spread(piece):
        left = lax.ppermute(piece[:UNIT], "dp", ring(8, 1))
        right = lax.ppermute(piece[UNIT:], "dp", ring(8, 7))
        pieces = (piece, left, right)
        return pieces + tuple(lax.ppermute(p, "core", SWAP) for p in pieces)

    far_2 = lax.ppermute(fetch_far(2), "yh", [(1, 0)])
    piece_3 = fetch_far(3)
    weights = [(own, other), (own, other), spread(far_2), None]
    block = swapped(after(cotangent[0], x))

    column = jnp.arange(D)
    wanted = (jnp.arange(MINE) // 24) * MINE + spot * 24 + jnp.arange(MINE) % 24
    pick = (column[None, :] == wanted[:, None]).astype(BF)

    saved = []
    qkv = first(0, where, x, weights[0])
    far_3 = lax.ppermute(after(piece_3, qkv), "yh", [(1, 0)])
    grad = gather_rows(after(block, qkv))
    for layer in range(4):
        kv = lax.ppermute(qkv[:, QW:], "core", SWAP)
        if layer == 3:
            att, tot = last(qkv, kv)
            saved.append((x, qkv, kv, att, tot))
            continue
        att, tot, out, *more = attend(layer, where, qkv, kv, x, weights[layer])
        saved.append((x, qkv, kv, att, tot))
        x = out
        qkv = more[0] if more else first(layer + 1, where, x, weights[layer + 1])
        if layer == 1:
            weights[3] = spread(after(far_3, qkv))

    def meet(first_terms, second_terms):
        keep = jnp.where(core == 0, first_terms, second_terms)
        give = jnp.where(core == 0, second_terms, first_terms)
        return (keep + lax.ppermute(give, "core", SWAP)).astype(BF)

    terms = [None] * 4
    far = None
    for layer in (3, 2, 1, 0):
        x, qkv, kv, att, tot = saved[layer]
        gq, own_part, far_part = score_grads(
            layer, where, grad, qkv, kv, att, tot, weights[layer]
        )
        got = lax.ppermute(far_part, "core", SWAP)
        grad, terms[layer] = input_grads(
            layer, where, own_part, got, gq, x, grad, att, pick, weights[layer]
        )
        if layer == 2:
            early = meet(terms[2], terms[3])
            grad, early = lax.optimization_barrier((grad, early))
            far = lax.ppermute(early, "yh", [(0, 1)])

    block = lax.dynamic_slice_in_dim(grad, lane * 128, 128, 0)
    even_part = jnp.concatenate([block[:, :384], block[:, 768:1152]], 1)
    odd_part = jnp.concatenate([block[:, 384:768], block[:, 1152:]], 1)
    to_other = jnp.where(core == 0, odd_part, even_part)
    kept = jnp.where(core == 0, even_part, odd_part)
    both = jnp.where(core == yl, kept, lax.ppermute(to_other, "core", SWAP))
    d_far = lax.ppermute(both[:, 384:], "yh", [(0, 1)])
    d_acts = jnp.where(yh == 0, both[:, :384], d_far)

    near = meet(terms[0], terms[1])
    payload = jnp.where(yh == 0, near, far).reshape(8, 24, TERMS)
    sums = jnp.sum(lax.all_to_all(payload, "dp", 0, 0).astype(F32), axis=0)
    return (
        d_acts[None],
        sums[:, ALL].reshape(1, 24),
        sums[None, :, :QW],
        sums[None, :, QW : 2 * QW],
        sums[None, :, 2 * QW : QKV],
        sums[None, :, QKV:ALL],
    )


def solution(mesh):
    fine = Mesh(mesh.devices.reshape(8, 2, 2, 2, 4), AXES)
    section = ("yh", "core")
    seq = ("yl", "x")
    rows = ("dp", "yl", "x")
    return jax.shard_map(
        program,
        mesh=fine,
        in_specs=(
            P("dp", seq, None),
            P("dp", seq, None),
            P(section, None),
            P(section, None, None),
            P(section, None, None),
            P(section, None, None),
            P(section, None, None),
        ),
        out_specs=(
            P("dp", seq, section),
            P(section, rows),
            P(section, rows, None),
            P(section, rows, None),
            P(section, rows, None),
            P(section, rows, None),
        ),
        check_vma=False,
    )
```

```python
import functools

import jax
import jax.numpy as jnp
from jax import lax
from jax.experimental import pallas as pl
from jax.experimental.pallas import tpu as pltpu
from jax.sharding import Mesh
from jax.sharding import PartitionSpec as P

HEADS = 4
KEY = 64
VALUE = 96
QW = HEADS * KEY
VW = HEADS * VALUE
KV = QW + VW
QKV = QW + KV
ALL = QKV + VW
D = 1536
UNIT = 208
TALL = 8 * UNIT
ROWS = 512
STEP = 256
MINE = 192
TERMS = ALL + 128
EPS = 1e-05
SCALE = KEY ** (-0.5)
BF = jnp.bfloat16
F32 = jnp.float32


AXES = ("dp", "yh", "core", "yl", "x")
SWAP = [(0, 1), (1, 0)]
HBM = pl.BlockSpec(memory_space=pltpu.HBM)
VMEM = pl.BlockSpec(memory_space=pltpu.VMEM)
SMEM = pl.BlockSpec(memory_space=pltpu.SMEM)


def dot(a, b):
    return lax.dot_general(a, b, (((1,), (0,)), ((), ())), preferred_element_type=F32)


def dot_t(a, b):
    return lax.dot_general(a, b, (((1,), (1,)), ((), ())), preferred_element_type=F32)


def lanes(width):
    return lax.broadcasted_iota(jnp.int32, (1, width), 1)


WINDOWS = ((0, 128), (0, 256), (128, 384), (256, 384))


def fetch(refs, layer, where, first, last, dst, sems):
    span = pl.ds(first, last - first)
    if layer < 2:
        on_own = where[0] == layer % 2
        own = pltpu.make_async_copy(refs[0].at[:, span], dst, sems.at[0])
        other = pltpu.make_async_copy(refs[1].at[:, span], dst, sems.at[0])
        pl.when(on_own)(own.start)
        pl.when(jnp.logical_not(on_own))(other.start)
        return own.wait
    core, odd = where[0], where[1]
    copies = []
    for k in range(2):
        near = 4 * odd + 2 * jnp.bitwise_xor(core, k)
        away = 4 * (1 - odd) + 2 * jnp.bitwise_xor(core, k)
        for j, (unit, count) in enumerate(((near, 2), (away, 1), (away + 1, 1))):
            start = pl.multiple_of(unit * UNIT, 16)
            copy = pltpu.make_async_copy(
                refs[3 * k + j].at[:, span],
                dst.at[pl.ds(start, count * UNIT)],
                sems.at[3 * k + j],
            )
            copy.start()
            copies.append(copy)
    return lambda: [copy.wait() for copy in copies]


def gain_row(w):
    return jnp.concatenate(
        [w[D : D + 1, :].astype(F32), w[D + 1 : D + 2, : D - QKV].astype(F32)], 1
    )


def norm(x):
    wide = x.astype(F32)
    centred = wide - jnp.mean(wide, axis=-1, keepdims=True)
    inverse = lax.rsqrt(jnp.mean(centred * centred, axis=-1, keepdims=True) + EPS)
    return centred * inverse, inverse


def project(x, gain, w):
    normed, _ = norm(x)
    return dot((normed * gain).astype(BF), w[:D, :]).astype(BF)


def head_query(q, h):
    mask = jnp.where(lanes(128) // KEY == h % 2, SCALE, 0.0).astype(BF)
    g = h // 2
    return q[:, 128 * g : 128 * g + 128] * mask


def build_kernel(where, wq_ref, wk_ref, wv_ref, wo_ref, gain_ref, own_ref, pick_ref, sems):
    copies = []
    at = 0
    for k, ref in enumerate((wq_ref, wk_ref, wv_ref, wo_ref)):
        width = ref.shape[2]
        copies.append(
            pltpu.make_async_copy(
                ref.at[0], own_ref.at[pl.ds(0, D), pl.ds(at, width)], sems.at[k]
            )
        )
        copies[-1].start()
        at += width
    gain = gain_ref[...].astype(F32)
    row = lax.broadcasted_iota(jnp.int32, (TALL - D, 1), 0)
    upper = jnp.concatenate([gain[:, :QKV], jnp.zeros((1, ALL - QKV), F32)], 1)
    lower = jnp.concatenate([gain[:, QKV:], jnp.zeros((1, ALL - D + QKV), F32)], 1)
    own_ref[D:, :] = jnp.where(row == 0, upper, jnp.where(row == 1, lower, 0.0)).astype(BF)
    column = lax.broadcasted_iota(jnp.int32, (24, D), 1)
    local = lax.broadcasted_iota(jnp.int32, (24, D), 0)
    for k in range(8):
        wanted = local + (MINE * k + 24 * where[3])
        pick_ref[24 * k : 24 * k + 24, :] = jnp.where(column == wanted, 1.0, 0.0).astype(BF)
    for copy in copies:
        copy.wait()


def halves_kernel(both_ref, low_ref, high_ref, sems):
    low = pltpu.make_async_copy(both_ref.at[pl.ds(0, UNIT)], low_ref, sems.at[0])
    high = pltpu.make_async_copy(both_ref.at[pl.ds(UNIT, UNIT)], high_ref, sems.at[1])
    low.start()
    high.start()
    low.wait()
    high.wait()


def join_kernel(where, keep_ref, got_ref, *rest):
    out_ref = rest[-1]
    total = (keep_ref[...] + got_ref[...]).astype(BF)
    if len(rest) == 2:
        total = jnp.where(where[4] == 0, total.astype(F32), rest[0][...].astype(F32)).astype(BF)
    out_ref[...] = total


def pieces_kernel(where, own_ref, other_ref, two_ref, three_ref, sems):
    start = pl.multiple_of((4 * where[1] + 2 * where[0]) * UNIT, 16)
    span = pl.ds(start, 2 * UNIT)

    def go(two, three):
        pltpu.make_async_copy(two.at[span], two_ref, sems.at[0]).start()
        pltpu.make_async_copy(three.at[span], three_ref, sems.at[1]).start()

    pl.when(where[0] == 0)(lambda: go(own_ref, other_ref))
    pl.when(where[0] == 1)(lambda: go(other_ref, own_ref))
    pltpu.make_async_copy(own_ref.at[span], two_ref, sems.at[0]).wait()
    pltpu.make_async_copy(own_ref.at[span], three_ref, sems.at[1]).wait()


def collect(parts, where, rows_ref, sems):
    copies = []
    for k, part in enumerate(parts):
        start = pl.multiple_of(((where[2] + 4 - k) % 4) * 128, 128)
        copies.append(
            pltpu.make_async_copy(part, rows_ref.at[pl.ds(start, 128)], sems.at[k])
        )
        copies[-1].start()
    return lambda: [copy.wait() for copy in copies]


def project_kernel(layer, where, *rest):
    if layer == 0:
        parts, rest = rest[:4], rest[4:]
        refs, (qkv_ref, x_ref, w, sems, sems_x) = rest[:-5], rest[-5:]
        ready_x = collect(parts, where, x_ref, sems_x)
    else:
        x_ref = rest[0]
        refs, (qkv_ref, w, sems) = rest[1:-3], rest[-3:]
    ready = fetch(refs, layer, where, 0, QKV, w, sems)
    if layer == 0:
        ready_x()
    ready()
    gain = gain_row(w)

    def step(i, carry):
        rows = pl.ds(pl.multiple_of(i * STEP, STEP), STEP)
        qkv_ref[rows, :] = project(x_ref[rows, :], gain, w)
        return carry

    lax.fori_loop(0, ROWS // STEP, step, 0)


def attend_kernel(layer, where, qkv_ref, kv_ref, x_ref, *rest):
    count = 2 if layer < 2 else 6
    refs, rest = rest[:count], rest[count:]
    if layer == 0:
        att_ref, tot_ref, out_ref, next_ref, wo, sems, w, sems_w = rest[-8:]
        ready_w = fetch(refs, 1, where, 0, QKV, w, sems_w)
    else:
        att_ref, tot_ref, out_ref, wo, sems = rest
    ready = fetch(refs, layer, where, QKV, ALL, wo, sems)

    def attend(i, carry):
        rows = pl.ds(pl.multiple_of(i * STEP, STEP), STEP)
        attention_step(rows, qkv_ref, kv_ref, att_ref, tot_ref)
        return carry

    lax.fori_loop(0, ROWS // STEP, attend, 0)
    ready()
    if layer == 0:
        ready_w()
        gain = gain_row(w)

    def finish(i, carry):
        rows = pl.ds(pl.multiple_of(i * STEP, STEP), STEP)
        mixed = dot_t(att_ref[rows, :], wo[:D, :])
        out = (x_ref[rows, :].astype(F32) + mixed).astype(BF)
        out_ref[rows, :] = out
        if layer == 0:
            next_ref[rows, :] = project(out, gain, w)
        return carry

    lax.fori_loop(0, ROWS // STEP, finish, 0)


def last_kernel(where, qkv_ref, kv_ref, *rest):
    parts, (att_ref, tot_ref, grad_ref, sems) = rest[:4], rest[4:]
    ready = collect(parts, where, grad_ref, sems)

    def attend(i, carry):
        attention_step(pl.ds(pl.multiple_of(i * STEP, STEP), STEP), qkv_ref, kv_ref, att_ref, tot_ref)
        return carry

    lax.fori_loop(0, ROWS // STEP, attend, 0)
    ready()


def attention_step(rows, qkv_ref, kv_ref, att_ref, tot_ref):
    q = qkv_ref[rows, :QW]
    attended = jnp.zeros((STEP, VW), F32)
    channel = lanes(VW) // VALUE
    for h in range(HEADS):
        g = 128 * (h // 2)
        qh = head_query(q, h)
        e_own = jnp.exp(dot_t(qh, qkv_ref[:, QW + g : QW + g + 128]))
        e_far = jnp.exp(dot_t(qh, kv_ref[:, g : g + 128]))
        total = jnp.sum(e_own + e_far, axis=-1, keepdims=True)
        lo, hi = WINDOWS[h]
        num = dot(e_own.astype(BF), qkv_ref[:, 2 * QW + lo : 2 * QW + hi]) + dot(
            e_far.astype(BF), kv_ref[:, QW + lo : QW + hi]
        )
        part = num / total
        pieces = []
        if lo:
            pieces.append(jnp.zeros((STEP, lo), F32))
        pieces.append(part)
        if hi < VW:
            pieces.append(jnp.zeros((STEP, VW - hi), F32))
        wide = jnp.concatenate(pieces, 1) if len(pieces) > 1 else part
        attended = jnp.where(channel == h, wide, attended)
        tot_ref[rows, h : h + 1] = total
    att_ref[rows, :] = attended.astype(BF)


def scores_kernel(layer, where, grad_ref, qkv_ref, kv_ref, att_ref, tot_ref, *rest):
    refs, (gq_ref, own_ref, far_ref, acc, wo, sems) = rest[:-6], rest[-6:]
    ready = fetch(refs, layer, where, QKV, ALL, wo, sems)
    acc[...] = jnp.zeros_like(acc)
    ready()
    channel = lanes(VW) // VALUE
    key_lane = lanes(128) // KEY

    def step(i, carry):
        rows = pl.ds(pl.multiple_of(i * STEP, STEP), STEP)
        grad = grad_ref[rows, :]
        g_att = dot(grad, wo[:D, :]).astype(BF)
        tot = tot_ref[rows, :]
        divisor = jnp.ones((STEP, VW), F32)
        for h in range(HEADS):
            divisor = jnp.where(channel == h, tot[:, h : h + 1], divisor)
        scaled_wide = (g_att.astype(F32) / divisor).astype(BF).astype(F32)
        scaled = scaled_wide.astype(BF)
        products = scaled_wide * att_ref[rows, :].astype(F32)
        scaled_t = scaled_wide.T.astype(BF)
        q = qkv_ref[rows, :QW]
        q_t = q.astype(F32).T.astype(BF)
        gq = [None, None]
        for h in range(HEADS):
            g = 128 * (h // 2)
            lo, hi = WINDOWS[h]
            corr = jnp.sum(jnp.where(channel == h, products, 0.0), axis=-1, keepdims=True)
            corr = corr.astype(BF).astype(F32)
            qh = head_query(q, h)
            sh = jnp.where(channel == h, scaled, jnp.zeros_like(scaled))[:, lo:hi]
            got = None
            for side in range(2):
                if side == 0:
                    k = qkv_ref[:, QW + g : QW + g + 128]
                    v = qkv_ref[:, 2 * QW + lo : 2 * QW + hi]
                else:
                    k = kv_ref[:, g : g + 128]
                    v = kv_ref[:, QW + lo : QW + hi]
                e = jnp.exp(dot_t(qh, k))
                gp = dot_t(sh, v)
                sg = (e * (gp - corr) * SCALE).astype(BF)
                more = dot(sg, k)
                got = more if got is None else got + more
                at = pl.ds(side * ROWS, ROWS)
                acc[KEY * h : KEY * h + KEY, at] += dot(q_t[KEY * h : KEY * h + KEY, :], sg)
                acc[QW + VALUE * h : QW + VALUE * h + VALUE, at] += dot(
                    scaled_t[VALUE * h : VALUE * h + VALUE, :], e.astype(BF)
                )
            p = h // 2
            gq[p] = got if h % 2 == 0 else jnp.where(key_lane == 1, got, gq[p])
        gq_ref[rows, :] = jnp.concatenate(gq, 1).astype(BF)
        return carry

    lax.fori_loop(0, ROWS // STEP, step, 0)
    own_ref[...] = acc[:, :ROWS]
    far_ref[...] = acc[:, ROWS:].astype(BF)


def inputs_kernel(layer, where, own_ref, got_ref, gq_ref, x_ref, grad_ref, att_ref, pick_ref, *rest):
    if layer % 2:
        refs, (pass_ref, term_ref, gqkv, normal, gg, w, sems) = rest[:-7], rest[-7:]
    else:
        prev_ref = rest[0]
        refs, (pass_ref, term_ref, give_ref, gqkv, normal, gg, w, sems) = rest[1:-8], rest[-8:]
    ready = fetch(refs, layer, where, 0, QKV, w, sems)
    gqkv[:, QW:] = (own_ref[...] + got_ref[...].astype(F32)).T.astype(BF)
    gqkv[:, :QW] = gq_ref[...]
    gg[...] = jnp.zeros_like(gg)
    ready()
    gain = gain_row(w)

    def step(i, carry):
        rows = pl.ds(pl.multiple_of(i * STEP, STEP), STEP)
        g = gqkv[rows, :]
        g_normal = dot_t(g, w[:D, :])
        normed, inverse = norm(x_ref[rows, :])
        normal[rows, :] = (normed * gain).astype(BF)
        gg[...] += jnp.sum(g_normal * normed, axis=0, keepdims=True)
        g_normed = g_normal * gain
        g_x = inverse * (
            g_normed
            - jnp.mean(g_normed, axis=-1, keepdims=True)
            - normed * jnp.mean(g_normed * normed, axis=-1, keepdims=True)
        )
        pass_ref[rows, :] = (grad_ref[rows, :].astype(F32) + g_x).astype(BF)
        return carry

    lax.fori_loop(0, ROWS // STEP, step, 0)
    pick = pick_ref[...]
    term_ref[:, :QKV] = dot(dot_t(pick, normal[...]).astype(BF), gqkv[...])
    term_ref[:, QKV:ALL] = dot(dot_t(pick, grad_ref[...]).astype(BF), att_ref[...])
    total = gg[...]
    high = total.astype(BF)
    low = (total - high.astype(F32)).astype(BF)
    both = jnp.concatenate(
        [jnp.broadcast_to(high, (64, D)), jnp.broadcast_to(low, (64, D))], 0
    )
    picked = dot_t(pick, both)
    term_ref[:, ALL:] = picked + pltpu.roll(picked, 64, 1)
    if layer % 2 == 0:
        @pl.when(where[0] == 0)
        def _():
            give_ref[...] = prev_ref[...]

        @pl.when(where[0] == 1)
        def _():
            give_ref[...] = term_ref[...]
            term_ref[...] = prev_ref[...]


def shape(*dims, dtype=BF):
    return jax.ShapeDtypeStruct(dims, dtype)


def call(kernel, out_shape, in_specs, scratch, limit=22):
    outs = jax.tree.map(lambda _: VMEM, out_shape)
    return pl.pallas_call(
        kernel,
        out_shape=out_shape,
        in_specs=in_specs,
        out_specs=outs,
        scratch_shapes=scratch,
        compiler_params=pltpu.CompilerParams(vmem_limit_bytes=limit << 20),
    )


W_IN = pltpu.VMEM((TALL, QKV), BF)
W_OUT = pltpu.VMEM((TALL, VW), BF)
SEMS = pltpu.SemaphoreType.DMA((6,))


def build(*args):
    return call(
        build_kernel,
        (shape(TALL, ALL), shape(MINE, D)),
        [SMEM] + [HBM] * 4 + [VMEM],
        [pltpu.SemaphoreType.DMA((4,))],
        12,
    )(*args)


def pieces(where, own, other):
    return pl.pallas_call(
        pieces_kernel,
        out_shape=(shape(2 * UNIT, ALL), shape(2 * UNIT, ALL)),
        in_specs=[SMEM, HBM, HBM],
        out_specs=(HBM, HBM),
        scratch_shapes=[pltpu.SemaphoreType.DMA((2,))],
        name="pieces",
        compiler_params=pltpu.CompilerParams(vmem_limit_bytes=4 << 20),
    )(where, own, other)


def halves(both):
    return pl.pallas_call(
        halves_kernel,
        out_shape=(shape(UNIT, ALL), shape(UNIT, ALL)),
        in_specs=[HBM],
        out_specs=(HBM, HBM),
        scratch_shapes=[pltpu.SemaphoreType.DMA((2,))],
        name="halves",
        compiler_params=pltpu.CompilerParams(vmem_limit_bytes=4 << 20),
    )(both)


def join(where, *terms):
    return call(
        join_kernel, shape(MINE, TERMS), [SMEM] + [VMEM] * len(terms), [], 8
    )(where, *terms)


def first(where, parts, ws):
    return call(
        functools.partial(project_kernel, 0),
        (shape(ROWS, QKV), shape(ROWS, D)),
        [SMEM] + [HBM] * (4 + len(ws)),
        [W_IN, SEMS, pltpu.SemaphoreType.DMA((4,))],
    )(where, *parts, *ws)


def later(layer, where, x, ws):
    return call(
        functools.partial(project_kernel, layer),
        shape(ROWS, QKV),
        [SMEM, VMEM] + [HBM] * len(ws),
        [W_IN, SEMS],
    )(where, x, *ws)


def attend(layer, where, qkv, kv, x, ws):
    out_shape = [shape(ROWS, VW), shape(ROWS, 128, dtype=F32), shape(ROWS, D)]
    scratch = [W_OUT, SEMS]
    if layer == 0:
        out_shape.append(shape(ROWS, QKV))
        scratch += [W_IN, SEMS]
    return call(
        functools.partial(attend_kernel, layer),
        out_shape,
        [SMEM, VMEM, VMEM, VMEM] + [HBM] * len(ws),
        scratch,
    )(where, qkv, kv, x, *ws)


def last(where, qkv, kv, parts):
    return call(
        last_kernel,
        (shape(ROWS, VW), shape(ROWS, 128, dtype=F32), shape(ROWS, D)),
        [SMEM, VMEM, VMEM] + [HBM] * 4,
        [pltpu.SemaphoreType.DMA((4,))],
    )(where, qkv, kv, *parts)


def score_grads(layer, where, grad, qkv, kv, att, tot, ws):
    return call(
        functools.partial(scores_kernel, layer),
        (shape(ROWS, QW), shape(KV, ROWS, dtype=F32), shape(KV, ROWS)),
        [SMEM] + [VMEM] * 5 + [HBM] * len(ws),
        [pltpu.VMEM((KV, 2 * ROWS), F32), W_OUT, SEMS],
    )(where, grad, qkv, kv, att, tot, *ws)


def input_grads(layer, where, own, got, gq, x, grad, att, pick, ws, prev):
    count = 1 if prev is None else 2
    return call(
        functools.partial(inputs_kernel, layer),
        (shape(ROWS, D),) + (shape(MINE, TERMS, dtype=F32),) * count,
        [SMEM] + [VMEM] * (6 + count) + [HBM] * len(ws),
        [
            pltpu.VMEM((ROWS, QKV), BF),
            pltpu.VMEM((ROWS, D), BF),
            pltpu.VMEM((1, D), F32),
            W_IN,
            SEMS,
        ],
    )(where, own, got, gq, x, grad, att, pick, *([] if prev is None else [prev]), *ws)


def after(value, *deps):
    return lax.optimization_barrier((value, *deps))[0]


def ring(count, k):
    return [(i, (i + k) % count) for i in range(count)]


def swapped(block):
    return lax.ppermute(block, ("core", "yl"), [(0, 0), (1, 2), (2, 1), (3, 3)])


def gather_rows(block):
    return [block] + [lax.ppermute(block, "x", ring(4, k)) for k in (1, 2, 3)]


def program(acts, cotangent, gains, w_query, w_key, w_value, w_out):
    core = lax.axis_index("core")
    yh = lax.axis_index("yh")
    yl = lax.axis_index("yl")
    lane = lax.axis_index("x")
    odd = lax.axis_index("dp") % 2
    where = jnp.stack([core, odd, lane, yl * 4 + lane, yh]).astype(jnp.int32)

    block = swapped(acts[0])
    cot = swapped(cotangent[0])
    own, pick = build(where, w_query, w_key, w_value, w_out, gains)
    other = lax.ppermute(own, "core", SWAP)
    x_parts = gather_rows(block)

    piece_2, piece_3 = pieces(where, own, other)

    def spread(piece):
        low, high = halves(piece)
        left = lax.ppermute(low, "dp", ring(8, 1))
        right = lax.ppermute(high, "dp", ring(8, 7))
        found = (piece, left, right)
        return found + tuple(lax.ppermute(p, "core", SWAP) for p in found)

    far_2 = lax.ppermute(piece_2, "yh", [(1, 0)])
    weights = [(own, other), (own, other), spread(far_2), None]

    saved = []
    qkv, x = first(where, x_parts, weights[0])
    far_3 = lax.ppermute(after(piece_3, qkv), "yh", [(1, 0)])
    grad_parts = gather_rows(after(cot, qkv))
    for layer in range(4):
        kv = lax.ppermute(qkv[:, QW:], "core", SWAP)
        if layer == 3:
            att, tot, grad = last(where, qkv, kv, grad_parts)
            saved.append((x, qkv, kv, att, tot))
            continue
        att, tot, out, *more = attend(layer, where, qkv, kv, x, weights[layer])
        saved.append((x, qkv, kv, att, tot))
        x = out
        qkv = more[0] if more else later(layer + 1, where, x, weights[layer + 1])
        if layer == 1:
            weights[3] = spread(after(far_3, qkv))

    terms = far_terms = None
    for layer in (3, 2, 1, 0):
        x, qkv, kv, att, tot = saved[layer]
        gq, own_part, far_part = score_grads(
            layer, where, grad, qkv, kv, att, tot, weights[layer]
        )
        got = lax.ppermute(far_part, "core", SWAP)
        prev = terms if layer % 2 == 0 else None
        grad, terms, *give = input_grads(
            layer, where, own_part, got, gq, x, grad, att, pick, weights[layer], prev
        )
        if layer % 2 == 0:
            met = lax.ppermute(give[0], "core", SWAP)
        if layer == 2:
            early = join(where, terms, met)
            far_terms = lax.ppermute(early, "yh", [(0, 1)])

    block = lax.dynamic_slice_in_dim(grad, lane * 128, 128, 0)
    even_part = jnp.concatenate([block[:, :384], block[:, 768:1152]], 1)
    odd_part = jnp.concatenate([block[:, 384:768], block[:, 1152:]], 1)
    to_other = jnp.where(core == 0, odd_part, even_part)
    kept = jnp.where(core == 0, even_part, odd_part)
    both = jnp.where(core == yl, kept, lax.ppermute(to_other, "core", SWAP))
    d_far = lax.ppermute(both[:, 384:], "yh", [(0, 1)])
    d_acts = jnp.where(yh == 0, both[:, :384], d_far)

    payload = join(where, terms, met, far_terms).reshape(8, 24, TERMS)
    sums = jnp.sum(lax.all_to_all(payload, "dp", 0, 0).astype(F32), axis=0)
    return (
        d_acts[None],
        sums[:, ALL].reshape(1, 24),
        sums[None, :, :QW],
        sums[None, :, QW : 2 * QW],
        sums[None, :, 2 * QW : QKV],
        sums[None, :, QKV:ALL],
    )


def solution(mesh):
    fine = Mesh(mesh.devices.reshape(8, 2, 2, 2, 4), AXES)
    section = ("yh", "core")
    seq = ("yl", "x")
    rows = ("dp", "yl", "x")
    return jax.shard_map(
        program,
        mesh=fine,
        in_specs=(
            P("dp", seq, None),
            P("dp", seq, None),
            P(section, None),
            P(section, None, None),
            P(section, None, None),
            P(section, None, None),
            P(section, None, None),
        ),
        out_specs=(
            P("dp", seq, section),
            P(section, rows),
            P(section, rows, None),
            P(section, rows, None),
            P(section, rows, None),
            P(section, rows, None),
        ),
        check_vma=False,
    )
```

```python
import functools

import jax
import jax.numpy as jnp
from jax import lax
from jax.experimental import pallas as pl
from jax.experimental.pallas import tpu as pltpu
from jax.sharding import Mesh
from jax.sharding import PartitionSpec as P

HEADS = 4
KEY = 64
VALUE = 96
QW = HEADS * KEY
VW = HEADS * VALUE
KV = QW + VW
QKV = QW + KV
ALL = QKV + VW
D = 1536
UNIT = 208
TALL = 8 * UNIT
ROWS = 512
STEP = 256
MINE = 192
TERMS = ALL + 128
EPS = 1e-05
SCALE = KEY ** (-0.5)
BF = jnp.bfloat16
F32 = jnp.float32


AXES = ("dp", "yh", "core", "yl", "x")
SWAP = [(0, 1), (1, 0)]
HBM = pl.BlockSpec(memory_space=pltpu.HBM)
VMEM = pl.BlockSpec(memory_space=pltpu.VMEM)
SMEM = pl.BlockSpec(memory_space=pltpu.SMEM)


def dot(a, b):
    return lax.dot_general(a, b, (((1,), (0,)), ((), ())), preferred_element_type=F32)


def dot_t(a, b):
    return lax.dot_general(a, b, (((1,), (1,)), ((), ())), preferred_element_type=F32)


def lanes(width):
    return lax.broadcasted_iota(jnp.int32, (1, width), 1)


WINDOWS = ((0, 128), (0, 256), (128, 384), (256, 384))


def fetch(refs, layer, where, first, last, dst, sems):
    span = pl.ds(first, last - first)
    if layer < 2:
        on_own = where[0] == layer % 2
        own = pltpu.make_async_copy(refs[0].at[:, span], dst, sems.at[0])
        other = pltpu.make_async_copy(refs[1].at[:, span], dst, sems.at[0])
        pl.when(on_own)(own.start)
        pl.when(jnp.logical_not(on_own))(other.start)
        return own.wait
    core, odd = where[0], where[1]
    copies = []
    for k in range(2):
        near = 4 * odd + 2 * jnp.bitwise_xor(core, k)
        away = 4 * (1 - odd) + 2 * jnp.bitwise_xor(core, k)
        for j, (unit, count) in enumerate(((near, 2), (away, 1), (away + 1, 1))):
            start = pl.multiple_of(unit * UNIT, 16)
            copy = pltpu.make_async_copy(
                refs[3 * k + j].at[:, span],
                dst.at[pl.ds(start, count * UNIT)],
                sems.at[3 * k + j],
            )
            copy.start()
            copies.append(copy)
    return lambda: [copy.wait() for copy in copies]


def gain_row(w):
    return jnp.concatenate(
        [w[D : D + 1, :].astype(F32), w[D + 1 : D + 2, : D - QKV].astype(F32)], 1
    )


def norm(x):
    wide = x.astype(F32)
    centred = wide - jnp.mean(wide, axis=-1, keepdims=True)
    inverse = lax.rsqrt(jnp.mean(centred * centred, axis=-1, keepdims=True) + EPS)
    return centred * inverse, inverse


def project(x, gain, w):
    normed, _ = norm(x)
    return dot((normed * gain).astype(BF), w[:D, :]).astype(BF)


def head_query(q, h):
    mask = jnp.where(lanes(128) // KEY == h % 2, SCALE, 0.0).astype(BF)
    g = h // 2
    return q[:, 128 * g : 128 * g + 128] * mask


def build_kernel(where, wq_ref, wk_ref, wv_ref, wo_ref, gain_ref, own_ref, pick_ref, sems):
    copies = []
    at = 0
    for k, ref in enumerate((wq_ref, wk_ref, wv_ref, wo_ref)):
        width = ref.shape[2]
        copies.append(
            pltpu.make_async_copy(
                ref.at[0], own_ref.at[pl.ds(0, D), pl.ds(at, width)], sems.at[k]
            )
        )
        copies[-1].start()
        at += width
    gain = gain_ref[...].astype(F32)
    row = lax.broadcasted_iota(jnp.int32, (TALL - D, 1), 0)
    upper = jnp.concatenate([gain[:, :QKV], jnp.zeros((1, ALL - QKV), F32)], 1)
    lower = jnp.concatenate([gain[:, QKV:], jnp.zeros((1, ALL - D + QKV), F32)], 1)
    own_ref[D:, :] = jnp.where(row == 0, upper, jnp.where(row == 1, lower, 0.0)).astype(BF)
    column = lax.broadcasted_iota(jnp.int32, (24, D), 1)
    local = lax.broadcasted_iota(jnp.int32, (24, D), 0)
    for k in range(8):
        wanted = local + (MINE * k + 24 * where[3])
        pick_ref[24 * k : 24 * k + 24, :] = jnp.where(column == wanted, 1.0, 0.0).astype(BF)
    for copy in copies:
        copy.wait()


def halves_kernel(both_ref, low_ref, high_ref, sems):
    low = pltpu.make_async_copy(both_ref.at[pl.ds(0, UNIT)], low_ref, sems.at[0])
    high = pltpu.make_async_copy(both_ref.at[pl.ds(UNIT, UNIT)], high_ref, sems.at[1])
    low.start()
    high.start()
    low.wait()
    high.wait()


def join_kernel(where, keep_ref, got_ref, *rest):
    out_ref = rest[-1]
    total = (keep_ref[...] + got_ref[...]).astype(BF)
    if len(rest) == 2:
        total = jnp.where(where[4] == 0, total.astype(F32), rest[0][...].astype(F32)).astype(BF)
    out_ref[...] = total


def pieces_kernel(where, own_ref, other_ref, two_ref, three_ref, sems):
    start = pl.multiple_of((4 * where[1] + 2 * where[0]) * UNIT, 16)
    span = pl.ds(start, 2 * UNIT)

    def go(two, three):
        pltpu.make_async_copy(two.at[span], two_ref, sems.at[0]).start()
        pltpu.make_async_copy(three.at[span], three_ref, sems.at[1]).start()

    pl.when(where[0] == 0)(lambda: go(own_ref, other_ref))
    pl.when(where[0] == 1)(lambda: go(other_ref, own_ref))
    pltpu.make_async_copy(own_ref.at[span], two_ref, sems.at[0]).wait()
    pltpu.make_async_copy(own_ref.at[span], three_ref, sems.at[1]).wait()


def collect(parts, where, rows_ref, sems):
    copies = []
    for k, part in enumerate(parts):
        start = pl.multiple_of(((where[2] + 4 - k) % 4) * 128, 128)
        copies.append(
            pltpu.make_async_copy(part, rows_ref.at[pl.ds(start, 128)], sems.at[k])
        )
        copies[-1].start()
    return lambda: [copy.wait() for copy in copies]


def project_kernel(layer, where, *rest):
    if layer == 0:
        parts, rest = rest[:4], rest[4:]
        refs, (qkv_ref, x_ref, w, sems, sems_x) = rest[:-5], rest[-5:]
        ready_x = collect(parts, where, x_ref, sems_x)
    else:
        x_ref = rest[0]
        refs, (qkv_ref, w, sems) = rest[1:-3], rest[-3:]
    ready = fetch(refs, layer, where, 0, QKV, w, sems)
    if layer == 0:
        ready_x()
    ready()
    gain = gain_row(w)

    def step(i, carry):
        rows = pl.ds(pl.multiple_of(i * STEP, STEP), STEP)
        qkv_ref[rows, :] = project(x_ref[rows, :], gain, w)
        return carry

    lax.fori_loop(0, ROWS // STEP, step, 0)


def attend_kernel(layer, where, qkv_ref, kv_ref, x_ref, *rest):
    count = 2 if layer < 2 else 6
    refs, rest = rest[:count], rest[count:]
    if layer == 0:
        att_ref, tot_ref, out_ref, next_ref, wo, sems, w, sems_w = rest[-8:]
        ready_w = fetch(refs, 1, where, 0, QKV, w, sems_w)
    else:
        att_ref, tot_ref, out_ref, wo, sems = rest
    ready = fetch(refs, layer, where, QKV, ALL, wo, sems)

    def attend(i, carry):
        rows = pl.ds(pl.multiple_of(i * STEP, STEP), STEP)
        attention_step(rows, qkv_ref, kv_ref, att_ref, tot_ref)
        return carry

    lax.fori_loop(0, ROWS // STEP, attend, 0)
    ready()
    if layer == 0:
        ready_w()
        gain = gain_row(w)

    def finish(i, carry):
        rows = pl.ds(pl.multiple_of(i * STEP, STEP), STEP)
        mixed = dot_t(att_ref[rows, :], wo[:D, :])
        out = (x_ref[rows, :].astype(F32) + mixed).astype(BF)
        out_ref[rows, :] = out
        if layer == 0:
            next_ref[rows, :] = project(out, gain, w)
        return carry

    lax.fori_loop(0, ROWS // STEP, finish, 0)


def last_kernel(where, qkv_ref, kv_ref, *rest):
    parts, (att_ref, tot_ref, grad_ref, sems) = rest[:4], rest[4:]
    ready = collect(parts, where, grad_ref, sems)

    def attend(i, carry):
        attention_step(pl.ds(pl.multiple_of(i * STEP, STEP), STEP), qkv_ref, kv_ref, att_ref, tot_ref)
        return carry

    lax.fori_loop(0, ROWS // STEP, attend, 0)
    ready()


def attention_step(rows, qkv_ref, kv_ref, att_ref, tot_ref):
    q = qkv_ref[rows, :QW]
    attended = jnp.zeros((STEP, VW), F32)
    channel = lanes(VW) // VALUE
    for h in range(HEADS):
        g = 128 * (h // 2)
        qh = head_query(q, h)
        e_own = jnp.exp(dot_t(qh, qkv_ref[:, QW + g : QW + g + 128]))
        e_far = jnp.exp(dot_t(qh, kv_ref[:, g : g + 128]))
        total = jnp.sum(e_own + e_far, axis=-1, keepdims=True)
        lo, hi = WINDOWS[h]
        num = dot(e_own.astype(BF), qkv_ref[:, 2 * QW + lo : 2 * QW + hi]) + dot(
            e_far.astype(BF), kv_ref[:, QW + lo : QW + hi]
        )
        part = num / total
        pieces = []
        if lo:
            pieces.append(jnp.zeros((STEP, lo), F32))
        pieces.append(part)
        if hi < VW:
            pieces.append(jnp.zeros((STEP, VW - hi), F32))
        wide = jnp.concatenate(pieces, 1) if len(pieces) > 1 else part
        attended = jnp.where(channel == h, wide, attended)
        tot_ref[rows, h : h + 1] = total
    att_ref[rows, :] = attended.astype(BF)


def side_step(rows, q, turned, scaled, corr, keys, values, acc):
    channel = lanes(VW) // VALUE
    gq = [None, None]
    for h in range(HEADS):
        p = h // 2
        lo, hi = WINDOWS[h]
        sh = jnp.where(channel == h, scaled, jnp.zeros_like(scaled))[:, lo:hi]
        k = keys(128 * p, 128 * p + 128)
        e = jnp.exp(dot_t(head_query(q, h), k))
        gp = dot_t(sh, values(lo, hi))
        sg = (e * (gp - corr[:, h : h + 1]) * SCALE).astype(BF)
        got = dot(sg, k)
        gq[p] = got if h % 2 == 0 else jnp.where(lanes(128) // KEY == 1, got, gq[p])
        at = pl.ds(KEY * h, KEY)
        acc[at, :] += dot(turned[at, rows], sg)
        at = pl.ds(QW + VALUE * h, VALUE)
        acc[at, :] += dot(turned[at, rows], e.astype(BF))
    return jnp.concatenate(gq, 1)


def far_scores_kernel(layer, where, grad_ref, qkv_ref, kv_ref, att_ref, tot_ref, *rest):
    refs, rest = rest[:-8], rest[-8:]
    gq_ref, far_ref, scaled_ref, corr_ref, turned_ref, acc, wo, sems = rest
    ready = fetch(refs, layer, where, QKV, ALL, wo, sems)
    acc[...] = jnp.zeros_like(acc)
    ready()
    channel = lanes(VW) // VALUE

    def step(i, carry):
        rows = pl.ds(pl.multiple_of(i * STEP, STEP), STEP)
        g_att = dot(grad_ref[rows, :], wo[:D, :]).astype(BF)
        tot = tot_ref[rows, :]
        divisor = jnp.ones((STEP, VW), F32)
        for h in range(HEADS):
            divisor = jnp.where(channel == h, tot[:, h : h + 1], divisor)
        scaled = (g_att.astype(F32) / divisor).astype(BF)
        wide = scaled.astype(F32)
        products = wide * att_ref[rows, :].astype(F32)
        q = qkv_ref[rows, :QW]
        turned_ref[:QW, rows] = q.astype(F32).T.astype(BF)
        turned_ref[QW:, rows] = wide.T.astype(BF)
        scaled_ref[rows, :] = scaled
        corr = jnp.zeros((STEP, 128), F32)
        for h in range(HEADS):
            one = jnp.sum(jnp.where(channel == h, products, 0.0), axis=-1, keepdims=True)
            corr = jnp.where(lanes(128) == h, one.astype(BF).astype(F32), corr)
        corr_ref[rows, :] = corr
        gq_ref[rows, :] = side_step(
            rows,
            q,
            turned_ref,
            scaled,
            corr,
            lambda lo, hi: kv_ref[:, lo:hi],
            lambda lo, hi: kv_ref[:, QW + lo : QW + hi],
            acc,
        )
        return carry

    lax.fori_loop(0, ROWS // STEP, step, 0)
    far_ref[...] = acc[...].astype(BF)


def own_scores_kernel(qkv_ref, part_ref, scaled_ref, corr_ref, turned_ref, gq_ref, own_ref):
    own_ref[...] = jnp.zeros_like(own_ref)

    def step(i, carry):
        rows = pl.ds(pl.multiple_of(i * STEP, STEP), STEP)
        more = side_step(
            rows,
            qkv_ref[rows, :QW],
            turned_ref,
            scaled_ref[rows, :],
            corr_ref[rows, :],
            lambda lo, hi: qkv_ref[:, QW + lo : QW + hi],
            lambda lo, hi: qkv_ref[:, 2 * QW + lo : 2 * QW + hi],
            own_ref,
        )
        gq_ref[rows, :] = (part_ref[rows, :] + more).astype(BF)
        return carry

    lax.fori_loop(0, ROWS // STEP, step, 0)


def inputs_kernel(layer, where, own_ref, got_ref, gq_ref, x_ref, grad_ref, att_ref, pick_ref, *rest):
    if layer % 2:
        refs, (pass_ref, term_ref, gqkv, normal, gg, w, sems) = rest[:-7], rest[-7:]
    else:
        prev_ref = rest[0]
        refs, (pass_ref, term_ref, give_ref, gqkv, normal, gg, w, sems) = rest[1:-8], rest[-8:]
    ready = fetch(refs, layer, where, 0, QKV, w, sems)
    gqkv[:, QW:] = (own_ref[...] + got_ref[...].astype(F32)).T.astype(BF)
    gqkv[:, :QW] = gq_ref[...]
    gg[...] = jnp.zeros_like(gg)
    ready()
    gain = gain_row(w)

    def step(i, carry):
        rows = pl.ds(pl.multiple_of(i * STEP, STEP), STEP)
        g = gqkv[rows, :]
        g_normal = dot_t(g, w[:D, :])
        normed, inverse = norm(x_ref[rows, :])
        normal[rows, :] = (normed * gain).astype(BF)
        gg[...] += jnp.sum(g_normal * normed, axis=0, keepdims=True)
        g_normed = g_normal * gain
        g_x = inverse * (
            g_normed
            - jnp.mean(g_normed, axis=-1, keepdims=True)
            - normed * jnp.mean(g_normed * normed, axis=-1, keepdims=True)
        )
        pass_ref[rows, :] = (grad_ref[rows, :].astype(F32) + g_x).astype(BF)
        return carry

    lax.fori_loop(0, ROWS // STEP, step, 0)
    pick = pick_ref[...]
    term_ref[:, :QKV] = dot(dot_t(pick, normal[...]).astype(BF), gqkv[...])
    term_ref[:, QKV:ALL] = dot(dot_t(pick, grad_ref[...]).astype(BF), att_ref[...])
    total = gg[...]
    high = total.astype(BF)
    low = (total - high.astype(F32)).astype(BF)
    both = jnp.concatenate(
        [jnp.broadcast_to(high, (64, D)), jnp.broadcast_to(low, (64, D))], 0
    )
    picked = dot_t(pick, both)
    term_ref[:, ALL:] = picked + pltpu.roll(picked, 64, 1)
    if layer % 2 == 0:
        @pl.when(where[0] == 0)
        def _():
            give_ref[...] = prev_ref[...]

        @pl.when(where[0] == 1)
        def _():
            give_ref[...] = term_ref[...]
            term_ref[...] = prev_ref[...]


def shape(*dims, dtype=BF):
    return jax.ShapeDtypeStruct(dims, dtype)


def call(kernel, out_shape, in_specs, scratch, limit=22):
    outs = jax.tree.map(lambda _: VMEM, out_shape)
    return pl.pallas_call(
        kernel,
        out_shape=out_shape,
        in_specs=in_specs,
        out_specs=outs,
        scratch_shapes=scratch,
        compiler_params=pltpu.CompilerParams(vmem_limit_bytes=limit << 20),
    )


W_IN = pltpu.VMEM((TALL, QKV), BF)
W_OUT = pltpu.VMEM((TALL, VW), BF)
SEMS = pltpu.SemaphoreType.DMA((6,))


def build(*args):
    return call(
        build_kernel,
        (shape(TALL, ALL), shape(MINE, D)),
        [SMEM] + [HBM] * 4 + [VMEM],
        [pltpu.SemaphoreType.DMA((4,))],
        12,
    )(*args)


def pieces(where, own, other):
    return pl.pallas_call(
        pieces_kernel,
        out_shape=(shape(2 * UNIT, ALL), shape(2 * UNIT, ALL)),
        in_specs=[SMEM, HBM, HBM],
        out_specs=(HBM, HBM),
        scratch_shapes=[pltpu.SemaphoreType.DMA((2,))],
        name="pieces",
        compiler_params=pltpu.CompilerParams(vmem_limit_bytes=4 << 20),
    )(where, own, other)


def halves(both):
    return pl.pallas_call(
        halves_kernel,
        out_shape=(shape(UNIT, ALL), shape(UNIT, ALL)),
        in_specs=[HBM],
        out_specs=(HBM, HBM),
        scratch_shapes=[pltpu.SemaphoreType.DMA((2,))],
        name="halves",
        compiler_params=pltpu.CompilerParams(vmem_limit_bytes=4 << 20),
    )(both)


def join(where, *terms):
    return call(
        join_kernel, shape(MINE, TERMS), [SMEM] + [VMEM] * len(terms), [], 8
    )(where, *terms)


def first(where, parts, ws):
    return call(
        functools.partial(project_kernel, 0),
        (shape(ROWS, QKV), shape(ROWS, D)),
        [SMEM] + [HBM] * (4 + len(ws)),
        [W_IN, SEMS, pltpu.SemaphoreType.DMA((4,))],
    )(where, *parts, *ws)


def later(layer, where, x, ws):
    return call(
        functools.partial(project_kernel, layer),
        shape(ROWS, QKV),
        [SMEM, VMEM] + [HBM] * len(ws),
        [W_IN, SEMS],
    )(where, x, *ws)


def attend(layer, where, qkv, kv, x, ws):
    out_shape = [shape(ROWS, VW), shape(ROWS, 128, dtype=F32), shape(ROWS, D)]
    scratch = [W_OUT, SEMS]
    if layer == 0:
        out_shape.append(shape(ROWS, QKV))
        scratch += [W_IN, SEMS]
    return call(
        functools.partial(attend_kernel, layer),
        out_shape,
        [SMEM, VMEM, VMEM, VMEM] + [HBM] * len(ws),
        scratch,
    )(where, qkv, kv, x, *ws)


def last(where, qkv, kv, parts):
    return call(
        last_kernel,
        (shape(ROWS, VW), shape(ROWS, 128, dtype=F32), shape(ROWS, D)),
        [SMEM, VMEM, VMEM] + [HBM] * 4,
        [pltpu.SemaphoreType.DMA((4,))],
    )(where, qkv, kv, *parts)


def far_scores(layer, where, grad, qkv, kv, att, tot, ws):
    return call(
        functools.partial(far_scores_kernel, layer),
        (
            shape(ROWS, QW, dtype=F32),
            shape(KV, ROWS),
            shape(ROWS, VW),
            shape(ROWS, 128, dtype=F32),
            shape(KV, ROWS),
        ),
        [SMEM] + [VMEM] * 5 + [HBM] * len(ws),
        [pltpu.VMEM((KV, ROWS), F32), W_OUT, SEMS],
    )(where, grad, qkv, kv, att, tot, *ws)


def own_scores(*args):
    return call(
        own_scores_kernel, (shape(ROWS, QW), shape(KV, ROWS, dtype=F32)), [VMEM] * 5, []
    )(*args)


def input_grads(layer, where, own, got, gq, x, grad, att, pick, ws, prev):
    count = 1 if prev is None else 2
    return call(
        functools.partial(inputs_kernel, layer),
        (shape(ROWS, D),) + (shape(MINE, TERMS, dtype=F32),) * count,
        [SMEM] + [VMEM] * (6 + count) + [HBM] * len(ws),
        [
            pltpu.VMEM((ROWS, QKV), BF),
            pltpu.VMEM((ROWS, D), BF),
            pltpu.VMEM((1, D), F32),
            W_IN,
            SEMS,
        ],
    )(where, own, got, gq, x, grad, att, pick, *([] if prev is None else [prev]), *ws)


def after(value, *deps):
    return lax.optimization_barrier((value, *deps))[0]


def ring(count, k):
    return [(i, (i + k) % count) for i in range(count)]


def swapped(block):
    return lax.ppermute(block, ("core", "yl"), [(0, 0), (1, 2), (2, 1), (3, 3)])


def gather_rows(block):
    return [block] + [lax.ppermute(block, "x", ring(4, k)) for k in (1, 2, 3)]


def in_hbm(*values):
    return [pltpu.with_memory_space_constraint(value, pltpu.HBM) for value in values]


def program(acts, cotangent, gains, w_query, w_key, w_value, w_out):
    core = lax.axis_index("core")
    yh = lax.axis_index("yh")
    yl = lax.axis_index("yl")
    lane = lax.axis_index("x")
    odd = lax.axis_index("dp") % 2
    where = jnp.stack([core, odd, lane, yl * 4 + lane, yh]).astype(jnp.int32)

    block = swapped(acts[0])
    cot = swapped(cotangent[0])
    own, pick = build(where, *in_hbm(w_query, w_key, w_value, w_out), gains)
    other = lax.ppermute(own, "core", SWAP)
    x_parts = gather_rows(block)

    piece_2, piece_3 = pieces(where, own, other)

    def spread(piece):
        low, high = halves(piece)
        left = lax.ppermute(low, "dp", ring(8, 1))
        right = lax.ppermute(high, "dp", ring(8, 7))
        found = (piece, left, right)
        return found + tuple(lax.ppermute(p, "core", SWAP) for p in found)

    far_2 = lax.ppermute(piece_2, "yh", [(1, 0)])
    weights = [(own, other), (own, other), spread(far_2), None]

    saved = []
    qkv, x = first(where, x_parts, weights[0])
    far_3 = lax.ppermute(after(piece_3, qkv), "yh", [(1, 0)])
    grad_parts = gather_rows(after(cot, qkv))
    for layer in range(4):
        kv = lax.ppermute(qkv[:, QW:], "core", SWAP)
        if layer == 3:
            att, tot, grad = last(where, qkv, kv, grad_parts)
            saved.append((x, qkv, kv, att, tot))
            continue
        att, tot, out, *more = attend(layer, where, qkv, kv, x, weights[layer])
        saved.append((x, qkv, kv, att, tot))
        x = out
        if layer == 1:
            weights[3] = spread(after(far_3, x))
        qkv = more[0] if more else later(layer + 1, where, x, weights[layer + 1])

    terms = far_terms = None
    for layer in (3, 2, 1, 0):
        x, qkv, kv, att, tot = saved[layer]
        part, far_part, scaled, corr, turned = far_scores(
            layer, where, grad, qkv, kv, att, tot, weights[layer]
        )
        got = lax.ppermute(far_part, "core", SWAP)
        gq, own_part = own_scores(qkv, part, scaled, corr, turned)
        prev = terms if layer % 2 == 0 else None
        grad, terms, *give = input_grads(
            layer, where, own_part, got, gq, x, grad, att, pick, weights[layer], prev
        )
        if layer % 2 == 0:
            met = lax.ppermute(give[0], "core", SWAP)
        if layer == 2:
            early = join(where, terms, met)
            far_terms = lax.ppermute(early, "yh", [(0, 1)])

    block = lax.dynamic_slice_in_dim(grad, lane * 128, 128, 0)
    even_part = jnp.concatenate([block[:, :384], block[:, 768:1152]], 1)
    odd_part = jnp.concatenate([block[:, 384:768], block[:, 1152:]], 1)
    to_other = jnp.where(core == 0, odd_part, even_part)
    kept = jnp.where(core == 0, even_part, odd_part)
    both = jnp.where(core == yl, kept, lax.ppermute(to_other, "core", SWAP))
    d_far = lax.ppermute(both[:, 384:], "yh", [(0, 1)])
    d_acts = jnp.where(yh == 0, both[:, :384], d_far)

    payload = join(where, terms, met, far_terms).reshape(8, 24, TERMS)
    sums = jnp.sum(lax.all_to_all(payload, "dp", 0, 0).astype(F32), axis=0)
    return (
        d_acts[None],
        sums[:, ALL].reshape(1, 24),
        sums[None, :, :QW],
        sums[None, :, QW : 2 * QW],
        sums[None, :, 2 * QW : QKV],
        sums[None, :, QKV:ALL],
    )


def solution(mesh):
    fine = Mesh(mesh.devices.reshape(8, 2, 2, 2, 4), AXES)
    section = ("yh", "core")
    seq = ("yl", "x")
    rows = ("dp", "yl", "x")
    return jax.shard_map(
        program,
        mesh=fine,
        in_specs=(
            P("dp", seq, None),
            P("dp", seq, None),
            P(section, None),
            P(section, None, None),
            P(section, None, None),
            P(section, None, None),
            P(section, None, None),
        ),
        out_specs=(
            P("dp", seq, section),
            P(section, rows),
            P(section, rows, None),
            P(section, rows, None),
            P(section, rows, None),
            P(section, rows, None),
        ),
        check_vma=False,
    )
```

```python
import functools

import jax
import jax.numpy as jnp
from jax import lax
from jax.experimental import pallas as pl
from jax.experimental.pallas import tpu as pltpu
from jax.sharding import Mesh
from jax.sharding import PartitionSpec as P

HEADS = 4
KEY = 64
VALUE = 96
QW = HEADS * KEY
VW = HEADS * VALUE
KV = QW + VW
QKV = QW + KV
ALL = QKV + VW
D = 1536
UNIT = 208
TALL = 8 * UNIT
ROWS = 512
STEP = 256
MINE = 192
TERMS = ALL + 128
EPS = 1e-05
SCALE = KEY ** (-0.5)
BF = jnp.bfloat16
F32 = jnp.float32


AXES = ("dp", "yh", "core", "yl", "x")
SWAP = [(0, 1), (1, 0)]
HBM = pl.BlockSpec(memory_space=pltpu.HBM)
VMEM = pl.BlockSpec(memory_space=pltpu.VMEM)
SMEM = pl.BlockSpec(memory_space=pltpu.SMEM)


def dot(a, b):
    return lax.dot_general(a, b, (((1,), (0,)), ((), ())), preferred_element_type=F32)


def dot_t(a, b):
    return lax.dot_general(a, b, (((1,), (1,)), ((), ())), preferred_element_type=F32)


def lanes(width):
    return lax.broadcasted_iota(jnp.int32, (1, width), 1)


WINDOWS = ((0, 128), (0, 256), (128, 384), (256, 384))


def fetch(refs, layer, where, first, last, dst, sems):
    span = pl.ds(first, last - first)
    if layer < 2:
        on_own = where[0] == layer % 2
        own = pltpu.make_async_copy(refs[0].at[:, span], dst, sems.at[0])
        other = pltpu.make_async_copy(refs[1].at[:, span], dst, sems.at[0])
        pl.when(on_own)(own.start)
        pl.when(jnp.logical_not(on_own))(other.start)
        return own.wait
    core, odd = where[0], where[1]
    copies = []
    for k in range(2):
        near = 4 * odd + 2 * jnp.bitwise_xor(core, k)
        away = 4 * (1 - odd) + 2 * jnp.bitwise_xor(core, k)
        for j, (unit, count) in enumerate(((near, 2), (away, 1), (away + 1, 1))):
            start = pl.multiple_of(unit * UNIT, 16)
            copy = pltpu.make_async_copy(
                refs[3 * k + j].at[:, span],
                dst.at[pl.ds(start, count * UNIT)],
                sems.at[3 * k + j],
            )
            copy.start()
            copies.append(copy)
    return lambda: [copy.wait() for copy in copies]


def gain_row(w):
    return jnp.concatenate(
        [w[D : D + 1, :].astype(F32), w[D + 1 : D + 2, : D - QKV].astype(F32)], 1
    )


def norm(x):
    wide = x.astype(F32)
    centred = wide - jnp.mean(wide, axis=-1, keepdims=True)
    inverse = lax.rsqrt(jnp.mean(centred * centred, axis=-1, keepdims=True) + EPS)
    return centred * inverse, inverse


def project(x, gain, w):
    normed, _ = norm(x)
    return dot((normed * gain).astype(BF), w[:D, :]).astype(BF)


def head_query(q, h):
    mask = jnp.where(lanes(128) // KEY == h % 2, SCALE, 0.0).astype(BF)
    g = h // 2
    return q[:, 128 * g : 128 * g + 128] * mask


def build_kernel(where, wq_ref, wk_ref, wv_ref, wo_ref, gain_ref, own_ref, pick_ref, sems):
    copies = []
    at = 0
    for k, ref in enumerate((wq_ref, wk_ref, wv_ref, wo_ref)):
        width = ref.shape[2]
        copies.append(
            pltpu.make_async_copy(
                ref.at[0], own_ref.at[pl.ds(0, D), pl.ds(at, width)], sems.at[k]
            )
        )
        copies[-1].start()
        at += width
    gain = gain_ref[...].astype(F32)
    row = lax.broadcasted_iota(jnp.int32, (TALL - D, 1), 0)
    upper = jnp.concatenate([gain[:, :QKV], jnp.zeros((1, ALL - QKV), F32)], 1)
    lower = jnp.concatenate([gain[:, QKV:], jnp.zeros((1, ALL - D + QKV), F32)], 1)
    own_ref[D:, :] = jnp.where(row == 0, upper, jnp.where(row == 1, lower, 0.0)).astype(BF)
    column = lax.broadcasted_iota(jnp.int32, (24, D), 1)
    local = lax.broadcasted_iota(jnp.int32, (24, D), 0)
    for k in range(8):
        wanted = local + (MINE * k + 24 * where[3])
        pick_ref[24 * k : 24 * k + 24, :] = jnp.where(column == wanted, 1.0, 0.0).astype(BF)
    for copy in copies:
        copy.wait()


def halves_kernel(both_ref, low_ref, high_ref, sems):
    low = pltpu.make_async_copy(both_ref.at[pl.ds(0, UNIT)], low_ref, sems.at[0])
    high = pltpu.make_async_copy(both_ref.at[pl.ds(UNIT, UNIT)], high_ref, sems.at[1])
    low.start()
    high.start()
    low.wait()
    high.wait()


def join_kernel(where, keep_ref, got_ref, *rest):
    out_ref = rest[-1]
    total = (keep_ref[...] + got_ref[...]).astype(BF)
    if len(rest) == 2:
        total = jnp.where(where[4] == 0, total.astype(F32), rest[0][...].astype(F32)).astype(BF)
    out_ref[...] = total


def pieces_kernel(where, own_ref, other_ref, two_ref, three_ref, sems):
    start = pl.multiple_of((4 * where[1] + 2 * where[0]) * UNIT, 16)
    span = pl.ds(start, 2 * UNIT)

    def go(two, three):
        pltpu.make_async_copy(two.at[span], two_ref, sems.at[0]).start()
        pltpu.make_async_copy(three.at[span], three_ref, sems.at[1]).start()

    pl.when(where[0] == 0)(lambda: go(own_ref, other_ref))
    pl.when(where[0] == 1)(lambda: go(other_ref, own_ref))
    pltpu.make_async_copy(own_ref.at[span], two_ref, sems.at[0]).wait()
    pltpu.make_async_copy(own_ref.at[span], three_ref, sems.at[1]).wait()


def collect(parts, where, rows_ref, sems):
    copies = []
    for k, part in enumerate(parts):
        start = pl.multiple_of(((where[2] + 4 - k) % 4) * 128, 128)
        copies.append(
            pltpu.make_async_copy(part, rows_ref.at[pl.ds(start, 128)], sems.at[k])
        )
        copies[-1].start()
    return lambda: [copy.wait() for copy in copies]


def project_kernel(layer, where, *rest):
    if layer == 0:
        parts, rest = rest[:4], rest[4:]
        refs, (qkv_ref, x_ref, w, sems, sems_x) = rest[:-5], rest[-5:]
        ready_x = collect(parts, where, x_ref, sems_x)
    else:
        x_ref = rest[0]
        refs, (qkv_ref, w, sems) = rest[1:-3], rest[-3:]
    ready = fetch(refs, layer, where, 0, QKV, w, sems)
    if layer == 0:
        ready_x()
    ready()
    gain = gain_row(w)

    def step(i, carry):
        rows = pl.ds(pl.multiple_of(i * STEP, STEP), STEP)
        qkv_ref[rows, :] = project(x_ref[rows, :], gain, w)
        return carry

    lax.fori_loop(0, ROWS // STEP, step, 0)


def attention_side(rows, qkv_ref, keys, values):
    q = qkv_ref[rows, :QW]
    num = jnp.zeros((STEP, VW), F32)
    totals = jnp.ones((STEP, 128), F32)
    for h in range(HEADS):
        g = 128 * (h // 2)
        lo, hi = WINDOWS[h]
        e = jnp.exp(dot_t(head_query(q, h), keys(g, g + 128)))
        total = jnp.sum(e, axis=-1, keepdims=True)
        totals = jnp.where(lanes(128) == h, total, totals)
        pieces = [dot(e.astype(BF), values(lo, hi))]
        if lo:
            pieces.insert(0, jnp.zeros((STEP, lo), F32))
        if hi < VW:
            pieces.append(jnp.zeros((STEP, VW - hi), F32))
        wide = jnp.concatenate(pieces, 1) if len(pieces) > 1 else pieces[0]
        num = jnp.where(lanes(VW) // VALUE == h, wide, num)
    return num, totals


def near_side(rows, qkv_ref):
    return attention_side(
        rows,
        qkv_ref,
        lambda lo, hi: qkv_ref[:, QW + lo : QW + hi],
        lambda lo, hi: qkv_ref[:, 2 * QW + lo : 2 * QW + hi],
    )


def finish_attention(rows, near, qkv_ref, kv_ref, att_ref, tot_ref):
    num, totals = attention_side(
        rows,
        qkv_ref,
        lambda lo, hi: kv_ref[:, lo:hi],
        lambda lo, hi: kv_ref[:, QW + lo : QW + hi],
    )
    num = num + near[0]
    totals = totals + near[1]
    divisor = jnp.ones((STEP, VW), F32)
    for h in range(HEADS):
        divisor = jnp.where(lanes(VW) // VALUE == h, totals[:, h : h + 1], divisor)
    att_ref[rows, :] = (num / divisor).astype(BF)
    tot_ref[rows, :] = totals


def near_kernel(qkv_ref, num_ref, sum_ref):
    def step(i, carry):
        rows = pl.ds(pl.multiple_of(i * STEP, STEP), STEP)
        num_ref[rows, :], sum_ref[rows, :] = near_side(rows, qkv_ref)
        return carry

    lax.fori_loop(0, ROWS // STEP, step, 0)


def attend_kernel(layer, where, qkv_ref, kv_ref, x_ref, *rest):
    if layer:
        num_ref, sum_ref, *rest = rest
    count = 2 if layer < 2 else 6
    refs, rest = rest[:count], rest[count:]
    if layer == 0:
        att_ref, tot_ref, out_ref, next_ref, wo, sems, w, sems_w = rest
        ready_w = fetch(refs, 1, where, 0, QKV, w, sems_w)
    else:
        att_ref, tot_ref, out_ref, wo, sems = rest
    ready = fetch(refs, layer, where, QKV, ALL, wo, sems)

    def attend(i, carry):
        rows = pl.ds(pl.multiple_of(i * STEP, STEP), STEP)
        near = (num_ref[rows, :], sum_ref[rows, :]) if layer else near_side(rows, qkv_ref)
        finish_attention(rows, near, qkv_ref, kv_ref, att_ref, tot_ref)
        return carry

    lax.fori_loop(0, ROWS // STEP, attend, 0)
    ready()
    if layer == 0:
        ready_w()
        gain = gain_row(w)

    def finish(i, carry):
        rows = pl.ds(pl.multiple_of(i * STEP, STEP), STEP)
        mixed = dot_t(att_ref[rows, :], wo[:D, :])
        out = (x_ref[rows, :].astype(F32) + mixed).astype(BF)
        out_ref[rows, :] = out
        if layer == 0:
            next_ref[rows, :] = project(out, gain, w)
        return carry

    lax.fori_loop(0, ROWS // STEP, finish, 0)


def last_kernel(where, qkv_ref, kv_ref, num_ref, sum_ref, *rest):
    parts, (att_ref, tot_ref, grad_ref, sems) = rest[:4], rest[4:]
    ready = collect(parts, where, grad_ref, sems)

    def attend(i, carry):
        rows = pl.ds(pl.multiple_of(i * STEP, STEP), STEP)
        near = (num_ref[rows, :], sum_ref[rows, :])
        finish_attention(rows, near, qkv_ref, kv_ref, att_ref, tot_ref)
        return carry

    lax.fori_loop(0, ROWS // STEP, attend, 0)
    ready()


def side_step(rows, q, turned, scaled, corr, keys, values, acc):
    channel = lanes(VW) // VALUE
    gq = [None, None]
    for h in range(HEADS):
        p = h // 2
        lo, hi = WINDOWS[h]
        sh = jnp.where(channel == h, scaled, jnp.zeros_like(scaled))[:, lo:hi]
        k = keys(128 * p, 128 * p + 128)
        e = jnp.exp(dot_t(head_query(q, h), k))
        gp = dot_t(sh, values(lo, hi))
        sg = (e * (gp - corr[:, h : h + 1]) * SCALE).astype(BF)
        got = dot(sg, k)
        gq[p] = got if h % 2 == 0 else jnp.where(lanes(128) // KEY == 1, got, gq[p])
        at = pl.ds(KEY * h, KEY)
        acc[at, :] += dot(turned[at, rows], sg)
        at = pl.ds(QW + VALUE * h, VALUE)
        acc[at, :] += dot(turned[at, rows], e.astype(BF))
    return jnp.concatenate(gq, 1)


def far_scores_kernel(layer, where, grad_ref, qkv_ref, kv_ref, att_ref, tot_ref, *rest):
    refs, rest = rest[:-8], rest[-8:]
    gq_ref, far_ref, scaled_ref, corr_ref, turned_ref, acc, wo, sems = rest
    ready = fetch(refs, layer, where, QKV, ALL, wo, sems)
    acc[...] = jnp.zeros_like(acc)
    ready()
    channel = lanes(VW) // VALUE

    def step(i, carry):
        rows = pl.ds(pl.multiple_of(i * STEP, STEP), STEP)
        g_att = dot(grad_ref[rows, :], wo[:D, :]).astype(BF)
        tot = tot_ref[rows, :]
        divisor = jnp.ones((STEP, VW), F32)
        for h in range(HEADS):
            divisor = jnp.where(channel == h, tot[:, h : h + 1], divisor)
        scaled = (g_att.astype(F32) / divisor).astype(BF)
        wide = scaled.astype(F32)
        products = wide * att_ref[rows, :].astype(F32)
        q = qkv_ref[rows, :QW]
        turned_ref[:QW, rows] = q.astype(F32).T.astype(BF)
        turned_ref[QW:, rows] = wide.T.astype(BF)
        scaled_ref[rows, :] = scaled
        corr = jnp.zeros((STEP, 128), F32)
        for h in range(HEADS):
            one = jnp.sum(jnp.where(channel == h, products, 0.0), axis=-1, keepdims=True)
            corr = jnp.where(lanes(128) == h, one.astype(BF).astype(F32), corr)
        corr_ref[rows, :] = corr
        gq_ref[rows, :] = side_step(
            rows,
            q,
            turned_ref,
            scaled,
            corr,
            lambda lo, hi: kv_ref[:, lo:hi],
            lambda lo, hi: kv_ref[:, QW + lo : QW + hi],
            acc,
        )
        return carry

    lax.fori_loop(0, ROWS // STEP, step, 0)
    far_ref[...] = acc[...].astype(BF)


def own_scores_kernel(qkv_ref, part_ref, scaled_ref, corr_ref, turned_ref, gq_ref, own_ref):
    own_ref[...] = jnp.zeros_like(own_ref)

    def step(i, carry):
        rows = pl.ds(pl.multiple_of(i * STEP, STEP), STEP)
        more = side_step(
            rows,
            qkv_ref[rows, :QW],
            turned_ref,
            scaled_ref[rows, :],
            corr_ref[rows, :],
            lambda lo, hi: qkv_ref[:, QW + lo : QW + hi],
            lambda lo, hi: qkv_ref[:, 2 * QW + lo : 2 * QW + hi],
            own_ref,
        )
        gq_ref[rows, :] = (part_ref[rows, :] + more).astype(BF)
        return carry

    lax.fori_loop(0, ROWS // STEP, step, 0)


def inputs_kernel(layer, where, own_ref, got_ref, gq_ref, x_ref, grad_ref, att_ref, pick_ref, *rest):
    if layer % 2:
        refs, (pass_ref, term_ref, gqkv, chosen, gg, w, sems) = rest[:-7], rest[-7:]
    else:
        prev_ref = rest[0]
        refs, (pass_ref, term_ref, give_ref, gqkv, chosen, gg, w, sems) = rest[1:-8], rest[-8:]
    ready = fetch(refs, layer, where, 0, QKV, w, sems)
    gqkv[:, QW:] = (own_ref[...] + got_ref[...].astype(F32)).T.astype(BF)
    gqkv[:, :QW] = gq_ref[...]
    gg[...] = jnp.zeros_like(gg)
    ready()
    gain = gain_row(w)
    pick = pick_ref[...]

    def step(i, carry):
        rows = pl.ds(pl.multiple_of(i * STEP, STEP), STEP)
        g = gqkv[rows, :]
        g_normal = dot_t(g, w[:D, :])
        normed, inverse = norm(x_ref[rows, :])
        grad = grad_ref[rows, :]
        chosen[0, :, rows] = dot_t(pick, (normed * gain).astype(BF)).astype(BF)
        chosen[1, :, rows] = dot_t(pick, grad).astype(BF)
        gg[...] += jnp.sum(g_normal * normed, axis=0, keepdims=True)
        g_normed = g_normal * gain
        g_x = inverse * (
            g_normed
            - jnp.mean(g_normed, axis=-1, keepdims=True)
            - normed * jnp.mean(g_normed * normed, axis=-1, keepdims=True)
        )
        pass_ref[rows, :] = (grad.astype(F32) + g_x).astype(BF)
        return carry

    lax.fori_loop(0, ROWS // STEP, step, 0)
    term_ref[:, :QKV] = dot(chosen[0], gqkv[...])
    term_ref[:, QKV:ALL] = dot(chosen[1], att_ref[...])
    total = gg[...]
    high = total.astype(BF)
    low = (total - high.astype(F32)).astype(BF)
    both = jnp.concatenate(
        [jnp.broadcast_to(high, (64, D)), jnp.broadcast_to(low, (64, D))], 0
    )
    picked = dot_t(pick, both)
    term_ref[:, ALL:] = picked + pltpu.roll(picked, 64, 1)
    if layer % 2 == 0:
        @pl.when(where[0] == 0)
        def _():
            give_ref[...] = prev_ref[...]

        @pl.when(where[0] == 1)
        def _():
            give_ref[...] = term_ref[...]
            term_ref[...] = prev_ref[...]


def shape(*dims, dtype=BF):
    return jax.ShapeDtypeStruct(dims, dtype)


def call(kernel, out_shape, in_specs, scratch, limit=18):
    outs = jax.tree.map(lambda _: VMEM, out_shape)
    return pl.pallas_call(
        kernel,
        out_shape=out_shape,
        in_specs=in_specs,
        out_specs=outs,
        scratch_shapes=scratch,
        compiler_params=pltpu.CompilerParams(vmem_limit_bytes=limit << 20),
    )


W_IN = pltpu.VMEM((TALL, QKV), BF)
W_OUT = pltpu.VMEM((TALL, VW), BF)
SEMS = pltpu.SemaphoreType.DMA((6,))


def build(*args):
    return call(
        build_kernel,
        (shape(TALL, ALL), shape(MINE, D)),
        [SMEM] + [HBM] * 4 + [VMEM],
        [pltpu.SemaphoreType.DMA((4,))],
        12,
    )(*args)


def pieces(where, own, other):
    return pl.pallas_call(
        pieces_kernel,
        out_shape=(shape(2 * UNIT, ALL), shape(2 * UNIT, ALL)),
        in_specs=[SMEM, HBM, HBM],
        out_specs=(HBM, HBM),
        scratch_shapes=[pltpu.SemaphoreType.DMA((2,))],
        name="pieces",
        compiler_params=pltpu.CompilerParams(vmem_limit_bytes=4 << 20),
    )(where, own, other)


def halves(both):
    return pl.pallas_call(
        halves_kernel,
        out_shape=(shape(UNIT, ALL), shape(UNIT, ALL)),
        in_specs=[HBM],
        out_specs=(HBM, HBM),
        scratch_shapes=[pltpu.SemaphoreType.DMA((2,))],
        name="halves",
        compiler_params=pltpu.CompilerParams(vmem_limit_bytes=4 << 20),
    )(both)


def join(where, *terms):
    return call(
        join_kernel, shape(MINE, TERMS), [SMEM] + [VMEM] * len(terms), [], 8
    )(where, *terms)


def first(where, parts, ws):
    return call(
        functools.partial(project_kernel, 0),
        (shape(ROWS, QKV), shape(ROWS, D)),
        [SMEM] + [HBM] * (4 + len(ws)),
        [W_IN, SEMS, pltpu.SemaphoreType.DMA((4,))],
    )(where, *parts, *ws)


def later(layer, where, x, ws):
    return call(
        functools.partial(project_kernel, layer),
        shape(ROWS, QKV),
        [SMEM, VMEM] + [HBM] * len(ws),
        [W_IN, SEMS],
    )(where, x, *ws)


def near_attention(qkv):
    return call(
        near_kernel,
        (shape(ROWS, VW, dtype=F32), shape(ROWS, 128, dtype=F32)),
        [VMEM],
        [],
    )(qkv)


def attend(layer, where, qkv, kv, x, near, ws):
    out_shape = [shape(ROWS, VW), shape(ROWS, 128, dtype=F32), shape(ROWS, D)]
    scratch = [W_OUT, SEMS]
    if layer == 0:
        out_shape.append(shape(ROWS, QKV))
        scratch += [W_IN, SEMS]
    return call(
        functools.partial(attend_kernel, layer),
        out_shape,
        [SMEM] + [VMEM] * (3 + len(near)) + [HBM] * len(ws),
        scratch,
    )(where, qkv, kv, x, *near, *ws)


def last(where, qkv, kv, near, parts):
    return call(
        last_kernel,
        (shape(ROWS, VW), shape(ROWS, 128, dtype=F32), shape(ROWS, D)),
        [SMEM] + [VMEM] * 4 + [HBM] * 4,
        [pltpu.SemaphoreType.DMA((4,))],
    )(where, qkv, kv, *near, *parts)


def far_scores(layer, where, grad, qkv, kv, att, tot, ws):
    return call(
        functools.partial(far_scores_kernel, layer),
        (
            shape(ROWS, QW, dtype=F32),
            shape(KV, ROWS),
            shape(ROWS, VW),
            shape(ROWS, 128, dtype=F32),
            shape(KV, ROWS),
        ),
        [SMEM] + [VMEM] * 5 + [HBM] * len(ws),
        [pltpu.VMEM((KV, ROWS), F32), W_OUT, SEMS],
    )(where, grad, qkv, kv, att, tot, *ws)


def own_scores(*args):
    return call(
        own_scores_kernel, (shape(ROWS, QW), shape(KV, ROWS, dtype=F32)), [VMEM] * 5, []
    )(*args)


def input_grads(layer, where, own, got, gq, x, grad, att, pick, ws, prev):
    count = 1 if prev is None else 2
    return call(
        functools.partial(inputs_kernel, layer),
        (shape(ROWS, D),) + (shape(MINE, TERMS, dtype=F32),) * count,
        [SMEM] + [VMEM] * (6 + count) + [HBM] * len(ws),
        [
            pltpu.VMEM((ROWS, QKV), BF),
            pltpu.VMEM((2, MINE, ROWS), BF),
            pltpu.VMEM((1, D), F32),
            W_IN,
            SEMS,
        ],
    )(where, own, got, gq, x, grad, att, pick, *([] if prev is None else [prev]), *ws)


def after(value, *deps):
    return lax.optimization_barrier((value, *deps))[0]


def ring(count, k):
    return [(i, (i + k) % count) for i in range(count)]


def swapped(block):
    return lax.ppermute(block, ("core", "yl"), [(0, 0), (1, 2), (2, 1), (3, 3)])


def gather_rows(block):
    return [block] + [lax.ppermute(block, "x", ring(4, k)) for k in (1, 2, 3)]


def in_hbm(*values):
    return [pltpu.with_memory_space_constraint(value, pltpu.HBM) for value in values]


def program(acts, cotangent, gains, w_query, w_key, w_value, w_out):
    core = lax.axis_index("core")
    yh = lax.axis_index("yh")
    yl = lax.axis_index("yl")
    lane = lax.axis_index("x")
    odd = lax.axis_index("dp") % 2
    where = jnp.stack([core, odd, lane, yl * 4 + lane, yh]).astype(jnp.int32)

    block = swapped(acts[0])
    cot = swapped(cotangent[0])
    own, pick = build(where, *in_hbm(w_query, w_key, w_value, w_out), gains)
    other = lax.ppermute(own, "core", SWAP)
    x_parts = gather_rows(block)

    piece_2, piece_3 = pieces(where, own, other)

    def spread(piece):
        low, high = halves(piece)
        left = lax.ppermute(low, "dp", ring(8, 1))
        right = lax.ppermute(high, "dp", ring(8, 7))
        found = (piece, left, right)
        return found + tuple(lax.ppermute(p, "core", SWAP) for p in found)

    far_2 = lax.ppermute(piece_2, "yh", [(1, 0)])
    weights = [(own, other), (own, other), spread(far_2), None]

    saved = []
    qkv, x = first(where, x_parts, weights[0])
    far_3 = lax.ppermute(after(piece_3, qkv), "yh", [(1, 0)])
    grad_parts = gather_rows(after(cot, qkv))
    for layer in range(4):
        kv = lax.ppermute(qkv[:, QW:], "core", SWAP)
        near = near_attention(qkv) if layer else ()
        if layer == 3:
            att, tot, grad = last(where, qkv, kv, near, grad_parts)
            saved.append((x, qkv, kv, att, tot))
            continue
        att, tot, out, *more = attend(layer, where, qkv, kv, x, near, weights[layer])
        saved.append((x, qkv, kv, att, tot))
        x = out
        if layer == 1:
            weights[3] = spread(after(far_3, x))
        qkv = more[0] if more else later(layer + 1, where, x, weights[layer + 1])

    terms = far_terms = None
    for layer in (3, 2, 1, 0):
        x, qkv, kv, att, tot = saved[layer]
        part, far_part, scaled, corr, turned = far_scores(
            layer, where, grad, qkv, kv, att, tot, weights[layer]
        )
        got = lax.ppermute(far_part, "core", SWAP)
        gq, own_part = own_scores(qkv, part, scaled, corr, turned)
        prev = terms if layer % 2 == 0 else None
        grad, terms, *give = input_grads(
            layer, where, own_part, got, gq, x, grad, att, pick, weights[layer], prev
        )
        if layer % 2 == 0:
            met = lax.ppermute(give[0], "core", SWAP)
        if layer == 2:
            early = join(where, terms, met)
            far_terms = lax.ppermute(early, "yh", [(0, 1)])

    block = lax.dynamic_slice_in_dim(grad, lane * 128, 128, 0)
    even_part = jnp.concatenate([block[:, :384], block[:, 768:1152]], 1)
    odd_part = jnp.concatenate([block[:, 384:768], block[:, 1152:]], 1)
    to_other = jnp.where(core == 0, odd_part, even_part)
    kept = jnp.where(core == 0, even_part, odd_part)
    both = jnp.where(core == yl, kept, lax.ppermute(to_other, "core", SWAP))
    d_far = lax.ppermute(both[:, 384:], "yh", [(0, 1)])
    d_acts = jnp.where(yh == 0, both[:, :384], d_far)

    payload = join(where, terms, met, far_terms).reshape(8, 24, TERMS)
    sums = jnp.sum(lax.all_to_all(payload, "dp", 0, 0).astype(F32), axis=0)
    return (
        d_acts[None],
        sums[:, ALL].reshape(1, 24),
        sums[None, :, :QW],
        sums[None, :, QW : 2 * QW],
        sums[None, :, 2 * QW : QKV],
        sums[None, :, QKV:ALL],
    )


def solution(mesh):
    fine = Mesh(mesh.devices.reshape(8, 2, 2, 2, 4), AXES)
    section = ("yh", "core")
    seq = ("yl", "x")
    rows = ("dp", "yl", "x")
    return jax.shard_map(
        program,
        mesh=fine,
        in_specs=(
            P("dp", seq, None),
            P("dp", seq, None),
            P(section, None),
            P(section, None, None),
            P(section, None, None),
            P(section, None, None),
            P(section, None, None),
        ),
        out_specs=(
            P("dp", seq, section),
            P(section, rows),
            P(section, rows, None),
            P(section, rows, None),
            P(section, rows, None),
            P(section, rows, None),
        ),
        check_vma=False,
    )
```

```python
import functools

import jax
import jax.numpy as jnp
from jax import lax
from jax.experimental import pallas as pl
from jax.experimental.pallas import tpu as pltpu
from jax.sharding import Mesh
from jax.sharding import PartitionSpec as P

HEADS = 4
KEY = 64
VALUE = 96
QW = HEADS * KEY
VW = HEADS * VALUE
KV = QW + VW
QKV = QW + KV
ALL = QKV + VW
D = 1536
UNIT = 208
TALL = 8 * UNIT
ROWS = 512
STEP = 256
MINE = 192
TERMS = ALL + 128
EPS = 1e-05
SCALE = KEY ** (-0.5)
BF = jnp.bfloat16
F32 = jnp.float32


AXES = ("dp", "yh", "core", "yl", "x")
SWAP = [(0, 1), (1, 0)]
HBM = pl.BlockSpec(memory_space=pltpu.HBM)
VMEM = pl.BlockSpec(memory_space=pltpu.VMEM)
SMEM = pl.BlockSpec(memory_space=pltpu.SMEM)


def dot(a, b):
    return lax.dot_general(a, b, (((1,), (0,)), ((), ())), preferred_element_type=F32)


def dot_t(a, b):
    return lax.dot_general(a, b, (((1,), (1,)), ((), ())), preferred_element_type=F32)


def lanes(width):
    return lax.broadcasted_iota(jnp.int32, (1, width), 1)


WINDOWS = ((0, 128), (0, 256), (128, 384), (256, 384))


def fetch(refs, layer, where, first, last, dst, sems):
    span = pl.ds(first, last - first)
    if layer < 2:
        on_own = where[0] == layer % 2
        own = pltpu.make_async_copy(refs[0].at[:, span], dst, sems.at[0])
        other = pltpu.make_async_copy(refs[1].at[:, span], dst, sems.at[0])
        pl.when(on_own)(own.start)
        pl.when(jnp.logical_not(on_own))(other.start)
        return own.wait
    core, odd = where[0], where[1]
    copies = []
    for k in range(2):
        near = 4 * odd + 2 * jnp.bitwise_xor(core, k)
        away = 4 * (1 - odd) + 2 * jnp.bitwise_xor(core, k)
        for j, (unit, count) in enumerate(((near, 2), (away, 1), (away + 1, 1))):
            start = pl.multiple_of(unit * UNIT, 16)
            copy = pltpu.make_async_copy(
                refs[3 * k + j].at[:, span],
                dst.at[pl.ds(start, count * UNIT)],
                sems.at[3 * k + j],
            )
            copy.start()
            copies.append(copy)
    return lambda: [copy.wait() for copy in copies]


def gain_row(w):
    return jnp.concatenate(
        [w[D : D + 1, :].astype(F32), w[D + 1 : D + 2, : D - QKV].astype(F32)], 1
    )


def norm(x):
    wide = x.astype(F32)
    centred = wide - jnp.mean(wide, axis=-1, keepdims=True)
    inverse = lax.rsqrt(jnp.mean(centred * centred, axis=-1, keepdims=True) + EPS)
    return centred * inverse, inverse


def project(x, gain, w):
    normed, _ = norm(x)
    return dot((normed * gain).astype(BF), w[:D, :]).astype(BF)


def head_query(q, h):
    mask = jnp.where(lanes(128) // KEY == h % 2, SCALE, 0.0).astype(BF)
    g = h // 2
    return q[:, 128 * g : 128 * g + 128] * mask


def build_kernel(where, wq_ref, wk_ref, wv_ref, wo_ref, gain_ref, own_ref, pick_ref, sems):
    copies = []
    at = 0
    for k, ref in enumerate((wq_ref, wk_ref, wv_ref, wo_ref)):
        width = ref.shape[2]
        copies.append(
            pltpu.make_async_copy(
                ref.at[0], own_ref.at[pl.ds(0, D), pl.ds(at, width)], sems.at[k]
            )
        )
        copies[-1].start()
        at += width
    gain = gain_ref[...].astype(F32)
    row = lax.broadcasted_iota(jnp.int32, (TALL - D, 1), 0)
    upper = jnp.concatenate([gain[:, :QKV], jnp.zeros((1, ALL - QKV), F32)], 1)
    lower = jnp.concatenate([gain[:, QKV:], jnp.zeros((1, ALL - D + QKV), F32)], 1)
    own_ref[D:, :] = jnp.where(row == 0, upper, jnp.where(row == 1, lower, 0.0)).astype(BF)
    column = lax.broadcasted_iota(jnp.int32, (24, D), 1)
    local = lax.broadcasted_iota(jnp.int32, (24, D), 0)
    for k in range(8):
        wanted = local + (MINE * k + 24 * where[3])
        pick_ref[24 * k : 24 * k + 24, :] = jnp.where(column == wanted, 1.0, 0.0).astype(BF)
    for copy in copies:
        copy.wait()


def halves_kernel(both_ref, low_ref, high_ref, sems):
    low = pltpu.make_async_copy(both_ref.at[pl.ds(0, UNIT)], low_ref, sems.at[0])
    high = pltpu.make_async_copy(both_ref.at[pl.ds(UNIT, UNIT)], high_ref, sems.at[1])
    low.start()
    high.start()
    low.wait()
    high.wait()


def join_kernel(where, keep_ref, got_ref, *rest):
    out_ref = rest[-1]
    total = (keep_ref[...] + got_ref[...].astype(F32)).astype(BF)
    if len(rest) == 2:
        total = jnp.where(where[4] == 0, total.astype(F32), rest[0][...].astype(F32)).astype(BF)
    out_ref[...] = total


def pieces_kernel(where, own_ref, other_ref, two_ref, three_ref, sems):
    start = pl.multiple_of((4 * where[1] + 2 * where[0]) * UNIT, 16)
    span = pl.ds(start, 2 * UNIT)

    def go(two, three):
        pltpu.make_async_copy(two.at[span], two_ref, sems.at[0]).start()
        pltpu.make_async_copy(three.at[span], three_ref, sems.at[1]).start()

    pl.when(where[0] == 0)(lambda: go(own_ref, other_ref))
    pl.when(where[0] == 1)(lambda: go(other_ref, own_ref))
    pltpu.make_async_copy(own_ref.at[span], two_ref, sems.at[0]).wait()
    pltpu.make_async_copy(own_ref.at[span], three_ref, sems.at[1]).wait()


def collect(parts, rows_ref, sems):
    copies = []
    for k, part in enumerate(parts):
        copies.append(
            pltpu.make_async_copy(part, rows_ref.at[pl.ds(128 * k, 128)], sems.at[k])
        )
        copies[-1].start()
    return lambda: [copy.wait() for copy in copies]


def early_kernel(where, *rest):
    parts, refs, (qkv_ref, w_ref, x, sems, sems_x) = rest[:2], rest[2:4], rest[4:]
    ready_x = collect(parts, x, sems_x)
    ready = fetch(refs, 0, where, 0, QKV, w_ref, sems)
    ready_x()
    ready()
    qkv_ref[...] = project(x[...], gain_row(w_ref), w_ref)


def project0_kernel(early_ref, w_ref, *rest):
    parts, (qkv_ref, x_ref, sems) = rest[:4], rest[4:]
    ready = collect(parts, x_ref, sems)
    qkv_ref[:STEP, :] = early_ref[...]
    ready()
    qkv_ref[STEP:, :] = project(x_ref[STEP:, :], gain_row(w_ref), w_ref)


def project_kernel(layer, where, x_ref, *rest):
    refs, (qkv_ref, w, sems) = rest[:-3], rest[-3:]
    fetch(refs, layer, where, 0, QKV, w, sems)()
    gain = gain_row(w)

    def step(i, carry):
        rows = pl.ds(pl.multiple_of(i * STEP, STEP), STEP)
        qkv_ref[rows, :] = project(x_ref[rows, :], gain, w)
        return carry

    lax.fori_loop(0, ROWS // STEP, step, 0)


def block_kernel(where, grad_ref, kept_ref, give_ref):
    block = grad_ref[:128, :]
    even = jnp.concatenate([block[:, :384], block[:, 768:1152]], 1)
    odd = jnp.concatenate([block[:, 384:768], block[:, 1152:]], 1)

    @pl.when(where[0] == 0)
    def _():
        kept_ref[...] = even
        give_ref[...] = odd

    @pl.when(where[0] == 1)
    def _():
        kept_ref[...] = odd
        give_ref[...] = even


def attention_side(rows, qkv_ref, keys, values):
    q = qkv_ref[rows, :QW]
    num = jnp.zeros((STEP, VW), F32)
    totals = jnp.ones((STEP, 128), F32)
    for h in range(HEADS):
        g = 128 * (h // 2)
        lo, hi = WINDOWS[h]
        e = jnp.exp(dot_t(head_query(q, h), keys(g, g + 128)))
        total = jnp.sum(e, axis=-1, keepdims=True)
        totals = jnp.where(lanes(128) == h, total, totals)
        pieces = [dot(e.astype(BF), values(lo, hi))]
        if lo:
            pieces.insert(0, jnp.zeros((STEP, lo), F32))
        if hi < VW:
            pieces.append(jnp.zeros((STEP, VW - hi), F32))
        wide = jnp.concatenate(pieces, 1) if len(pieces) > 1 else pieces[0]
        num = jnp.where(lanes(VW) // VALUE == h, wide, num)
    return num, totals


def near_side(rows, qkv_ref):
    return attention_side(
        rows,
        qkv_ref,
        lambda lo, hi: qkv_ref[:, QW + lo : QW + hi],
        lambda lo, hi: qkv_ref[:, 2 * QW + lo : 2 * QW + hi],
    )


def finish_attention(rows, near, qkv_ref, kv_ref, att_ref, tot_ref):
    num, totals = attention_side(
        rows,
        qkv_ref,
        lambda lo, hi: kv_ref[:, lo:hi],
        lambda lo, hi: kv_ref[:, QW + lo : QW + hi],
    )
    num = num + near[0]
    totals = totals + near[1]
    divisor = jnp.ones((STEP, VW), F32)
    for h in range(HEADS):
        divisor = jnp.where(lanes(VW) // VALUE == h, totals[:, h : h + 1], divisor)
    att_ref[rows, :] = (num / divisor).astype(BF)
    tot_ref[rows, :] = totals


def near_kernel(qkv_ref, num_ref, sum_ref):
    def step(i, carry):
        rows = pl.ds(pl.multiple_of(i * STEP, STEP), STEP)
        num_ref[rows, :], sum_ref[rows, :] = near_side(rows, qkv_ref)
        return carry

    lax.fori_loop(0, ROWS // STEP, step, 0)


def attend_kernel(layer, where, qkv_ref, kv_ref, x_ref, *rest):
    if layer:
        num_ref, sum_ref, *rest = rest
    count = 2 if layer < 2 else 6
    refs, rest = rest[:count], rest[count:]
    if layer == 0:
        att_ref, tot_ref, out_ref, next_ref, wo, sems, w, sems_w = rest
        ready_w = fetch(refs, 1, where, 0, QKV, w, sems_w)
    else:
        att_ref, tot_ref, out_ref, wo, sems = rest
    ready = fetch(refs, layer, where, QKV, ALL, wo, sems)

    def attend(i, carry):
        rows = pl.ds(pl.multiple_of(i * STEP, STEP), STEP)
        near = (num_ref[rows, :], sum_ref[rows, :]) if layer else near_side(rows, qkv_ref)
        finish_attention(rows, near, qkv_ref, kv_ref, att_ref, tot_ref)
        return carry

    lax.fori_loop(0, ROWS // STEP, attend, 0)
    ready()
    if layer == 0:
        ready_w()
        gain = gain_row(w)

    def finish(i, carry):
        rows = pl.ds(pl.multiple_of(i * STEP, STEP), STEP)
        mixed = dot_t(att_ref[rows, :], wo[:D, :])
        out = (x_ref[rows, :].astype(F32) + mixed).astype(BF)
        out_ref[rows, :] = out
        if layer == 0:
            next_ref[rows, :] = project(out, gain, w)
        return carry

    lax.fori_loop(0, ROWS // STEP, finish, 0)


def last_kernel(where, qkv_ref, kv_ref, num_ref, sum_ref, *rest):
    parts, (att_ref, tot_ref, grad_ref, sems) = rest[:4], rest[4:]
    ready = collect(parts, grad_ref, sems)

    def attend(i, carry):
        rows = pl.ds(pl.multiple_of(i * STEP, STEP), STEP)
        near = (num_ref[rows, :], sum_ref[rows, :])
        finish_attention(rows, near, qkv_ref, kv_ref, att_ref, tot_ref)
        return carry

    lax.fori_loop(0, ROWS // STEP, attend, 0)
    ready()


def side_step(rows, q, turned, scaled, corr, keys, values, acc):
    channel = lanes(VW) // VALUE
    gq = [None, None]
    for h in range(HEADS):
        p = h // 2
        lo, hi = WINDOWS[h]
        sh = jnp.where(channel == h, scaled, jnp.zeros_like(scaled))[:, lo:hi]
        k = keys(128 * p, 128 * p + 128)
        e = jnp.exp(dot_t(head_query(q, h), k))
        gp = dot_t(sh, values(lo, hi))
        sg = (e * (gp - corr[:, h : h + 1]) * SCALE).astype(BF)
        got = dot(sg, k)
        gq[p] = got if h % 2 == 0 else jnp.where(lanes(128) // KEY == 1, got, gq[p])
        at = pl.ds(KEY * h, KEY)
        acc[at, :] += dot(turned[at, rows], sg)
        at = pl.ds(QW + VALUE * h, VALUE)
        acc[at, :] += dot(turned[at, rows], e.astype(BF))
    return jnp.concatenate(gq, 1)


def far_scores_kernel(layer, where, grad_ref, qkv_ref, kv_ref, att_ref, tot_ref, *rest):
    refs, rest = rest[:-8], rest[-8:]
    gq_ref, far_ref, scaled_ref, corr_ref, turned_ref, acc, wo, sems = rest
    ready = fetch(refs, layer, where, QKV, ALL, wo, sems)
    acc[...] = jnp.zeros_like(acc)
    ready()
    channel = lanes(VW) // VALUE

    def step(i, carry):
        rows = pl.ds(pl.multiple_of(i * STEP, STEP), STEP)
        g_att = dot(grad_ref[rows, :], wo[:D, :]).astype(BF)
        tot = tot_ref[rows, :]
        divisor = jnp.ones((STEP, VW), F32)
        for h in range(HEADS):
            divisor = jnp.where(channel == h, tot[:, h : h + 1], divisor)
        scaled = (g_att.astype(F32) / divisor).astype(BF)
        wide = scaled.astype(F32)
        products = wide * att_ref[rows, :].astype(F32)
        q = qkv_ref[rows, :QW]
        turned_ref[:QW, rows] = q.astype(F32).T.astype(BF)
        turned_ref[QW:, rows] = wide.T.astype(BF)
        scaled_ref[rows, :] = scaled
        corr = jnp.zeros((STEP, 128), F32)
        for h in range(HEADS):
            one = jnp.sum(jnp.where(channel == h, products, 0.0), axis=-1, keepdims=True)
            corr = jnp.where(lanes(128) == h, one.astype(BF).astype(F32), corr)
        corr_ref[rows, :] = corr
        gq_ref[rows, :] = side_step(
            rows,
            q,
            turned_ref,
            scaled,
            corr,
            lambda lo, hi: kv_ref[:, lo:hi],
            lambda lo, hi: kv_ref[:, QW + lo : QW + hi],
            acc,
        )
        return carry

    lax.fori_loop(0, ROWS // STEP, step, 0)
    far_ref[...] = acc[...].astype(BF)


def own_scores_kernel(qkv_ref, part_ref, scaled_ref, corr_ref, turned_ref, gq_ref, own_ref):
    own_ref[...] = jnp.zeros_like(own_ref)

    def step(i, carry):
        rows = pl.ds(pl.multiple_of(i * STEP, STEP), STEP)
        more = side_step(
            rows,
            qkv_ref[rows, :QW],
            turned_ref,
            scaled_ref[rows, :],
            corr_ref[rows, :],
            lambda lo, hi: qkv_ref[:, QW + lo : QW + hi],
            lambda lo, hi: qkv_ref[:, 2 * QW + lo : 2 * QW + hi],
            own_ref,
        )
        gq_ref[rows, :] = (part_ref[rows, :] + more).astype(BF)
        return carry

    lax.fori_loop(0, ROWS // STEP, step, 0)


def inputs_kernel(layer, where, own_ref, got_ref, gq_ref, x_ref, grad_ref, att_ref, pick_ref, *rest):
    if layer % 2:
        refs, (pass_ref, term_ref, gqkv, chosen, gg, w, sems) = rest[:-7], rest[-7:]
    else:
        prev_ref = rest[0]
        refs, (pass_ref, term_ref, give_ref, gqkv, chosen, gg, w, sems) = rest[1:-8], rest[-8:]
    ready = fetch(refs, layer, where, 0, QKV, w, sems)
    gqkv[:, QW:] = (own_ref[...] + got_ref[...].astype(F32)).T.astype(BF)
    gqkv[:, :QW] = gq_ref[...]
    gg[...] = jnp.zeros_like(gg)
    ready()
    gain = gain_row(w)
    pick = pick_ref[...]

    def step(i, carry):
        rows = pl.ds(pl.multiple_of(i * STEP, STEP), STEP)
        g = gqkv[rows, :]
        g_normal = dot_t(g, w[:D, :])
        normed, inverse = norm(x_ref[rows, :])
        grad = grad_ref[rows, :]
        chosen[0, :, rows] = dot_t(pick, (normed * gain).astype(BF)).astype(BF)
        chosen[1, :, rows] = dot_t(pick, grad).astype(BF)
        gg[...] += jnp.sum(g_normal * normed, axis=0, keepdims=True)
        g_normed = g_normal * gain
        g_x = inverse * (
            g_normed
            - jnp.mean(g_normed, axis=-1, keepdims=True)
            - normed * jnp.mean(g_normed * normed, axis=-1, keepdims=True)
        )
        pass_ref[rows, :] = (grad.astype(F32) + g_x).astype(BF)
        return carry

    lax.fori_loop(0, ROWS // STEP, step, 0)
    term_ref[:, :QKV] = dot(chosen[0], gqkv[...])
    term_ref[:, QKV:ALL] = dot(chosen[1], att_ref[...])
    total = gg[...]
    high = total.astype(BF)
    low = (total - high.astype(F32)).astype(BF)
    both = jnp.concatenate(
        [jnp.broadcast_to(high, (64, D)), jnp.broadcast_to(low, (64, D))], 0
    )
    picked = dot_t(pick, both)
    term_ref[:, ALL:] = picked + pltpu.roll(picked, 64, 1)
    if layer % 2 == 0:
        @pl.when(where[0] == 0)
        def _():
            give_ref[...] = prev_ref[...].astype(BF)

        @pl.when(where[0] == 1)
        def _():
            give_ref[...] = term_ref[...].astype(BF)
            term_ref[...] = prev_ref[...]


def shape(*dims, dtype=BF):
    return jax.ShapeDtypeStruct(dims, dtype)


def call(kernel, out_shape, in_specs, scratch, limit=18):
    outs = jax.tree.map(lambda _: VMEM, out_shape)
    return pl.pallas_call(
        kernel,
        out_shape=out_shape,
        in_specs=in_specs,
        out_specs=outs,
        scratch_shapes=scratch,
        compiler_params=pltpu.CompilerParams(vmem_limit_bytes=limit << 20),
    )


W_IN = pltpu.VMEM((TALL, QKV), BF)
W_OUT = pltpu.VMEM((TALL, VW), BF)
SEMS = pltpu.SemaphoreType.DMA((6,))


def build(*args):
    return call(
        build_kernel,
        (shape(TALL, ALL), shape(MINE, D)),
        [SMEM] + [HBM] * 4 + [VMEM],
        [pltpu.SemaphoreType.DMA((4,))],
        12,
    )(*args)


def pieces(where, own, other):
    return pl.pallas_call(
        pieces_kernel,
        out_shape=(shape(2 * UNIT, ALL), shape(2 * UNIT, ALL)),
        in_specs=[SMEM, HBM, HBM],
        out_specs=(HBM, HBM),
        scratch_shapes=[pltpu.SemaphoreType.DMA((2,))],
        name="pieces",
        compiler_params=pltpu.CompilerParams(vmem_limit_bytes=4 << 20),
    )(where, own, other)


def halves(both):
    return pl.pallas_call(
        halves_kernel,
        out_shape=(shape(UNIT, ALL), shape(UNIT, ALL)),
        in_specs=[HBM],
        out_specs=(HBM, HBM),
        scratch_shapes=[pltpu.SemaphoreType.DMA((2,))],
        name="halves",
        compiler_params=pltpu.CompilerParams(vmem_limit_bytes=4 << 20),
    )(both)


def join(where, *terms):
    return call(
        join_kernel, shape(MINE, TERMS), [SMEM] + [VMEM] * len(terms), [], 8
    )(where, *terms)


def first(where, parts, ws):
    early, w = call(
        early_kernel,
        (shape(STEP, QKV), shape(TALL, QKV)),
        [SMEM] + [HBM] * 4,
        [pltpu.VMEM((STEP, D), BF), SEMS, pltpu.SemaphoreType.DMA((2,))],
    )(where, *parts[:2], *ws)
    return call(
        project0_kernel,
        (shape(ROWS, QKV), shape(ROWS, D)),
        [VMEM, VMEM] + [HBM] * 4,
        [pltpu.SemaphoreType.DMA((4,))],
    )(early, w, *parts)


def own_block(where, grad):
    return call(
        block_kernel, (shape(128, 768), shape(128, 768)), [SMEM, VMEM], [], 8
    )(where, grad)


def later(layer, where, x, ws):
    return call(
        functools.partial(project_kernel, layer),
        shape(ROWS, QKV),
        [SMEM, VMEM] + [HBM] * len(ws),
        [W_IN, SEMS],
    )(where, x, *ws)


def near_attention(qkv):
    return call(
        near_kernel,
        (shape(ROWS, VW, dtype=F32), shape(ROWS, 128, dtype=F32)),
        [VMEM],
        [],
    )(qkv)


def attend(layer, where, qkv, kv, x, near, ws):
    out_shape = [shape(ROWS, VW), shape(ROWS, 128, dtype=F32), shape(ROWS, D)]
    scratch = [W_OUT, SEMS]
    if layer == 0:
        out_shape.append(shape(ROWS, QKV))
        scratch += [W_IN, SEMS]
    return call(
        functools.partial(attend_kernel, layer),
        out_shape,
        [SMEM] + [VMEM] * (3 + len(near)) + [HBM] * len(ws),
        scratch,
    )(where, qkv, kv, x, *near, *ws)


def last(where, qkv, kv, near, parts):
    return call(
        last_kernel,
        (shape(ROWS, VW), shape(ROWS, 128, dtype=F32), shape(ROWS, D)),
        [SMEM] + [VMEM] * 4 + [HBM] * 4,
        [pltpu.SemaphoreType.DMA((4,))],
    )(where, qkv, kv, *near, *parts)


def far_scores(layer, where, grad, qkv, kv, att, tot, ws):
    return call(
        functools.partial(far_scores_kernel, layer),
        (
            shape(ROWS, QW, dtype=F32),
            shape(KV, ROWS),
            shape(ROWS, VW),
            shape(ROWS, 128, dtype=F32),
            shape(KV, ROWS),
        ),
        [SMEM] + [VMEM] * 5 + [HBM] * len(ws),
        [pltpu.VMEM((KV, ROWS), F32), W_OUT, SEMS],
    )(where, grad, qkv, kv, att, tot, *ws)


def own_scores(*args):
    return call(
        own_scores_kernel, (shape(ROWS, QW), shape(KV, ROWS, dtype=F32)), [VMEM] * 5, []
    )(*args)


def input_grads(layer, where, own, got, gq, x, grad, att, pick, ws, prev):
    count = 1 if prev is None else 2
    return call(
        functools.partial(inputs_kernel, layer),
        (shape(ROWS, D), shape(MINE, TERMS, dtype=F32)) + (shape(MINE, TERMS),) * (count - 1),
        [SMEM] + [VMEM] * (6 + count) + [HBM] * len(ws),
        [
            pltpu.VMEM((ROWS, QKV), BF),
            pltpu.VMEM((2, MINE, ROWS), BF),
            pltpu.VMEM((1, D), F32),
            W_IN,
            SEMS,
        ],
    )(where, own, got, gq, x, grad, att, pick, *([] if prev is None else [prev]), *ws)


def after(value, *deps):
    return lax.optimization_barrier((value, *deps))[0]


def ring(count, k):
    return [(i, (i + k) % count) for i in range(count)]


def swapped(block):
    return lax.ppermute(block, ("core", "yl"), [(0, 0), (1, 2), (2, 1), (3, 3)])


def gather_rows(block):
    return [block] + [lax.ppermute(block, "x", ring(4, k)) for k in (1, 2, 3)]


def in_hbm(*values):
    return [pltpu.with_memory_space_constraint(value, pltpu.HBM) for value in values]


def program(acts, cotangent, gains, w_query, w_key, w_value, w_out):
    core = lax.axis_index("core")
    yh = lax.axis_index("yh")
    yl = lax.axis_index("yl")
    lane = lax.axis_index("x")
    odd = lax.axis_index("dp") % 2
    where = jnp.stack([core, odd, lane, yl * 4 + lane, yh]).astype(jnp.int32)

    block = swapped(acts[0])
    cot = swapped(cotangent[0])
    own, pick = build(where, *in_hbm(w_query, w_key, w_value, w_out), gains)
    other = lax.ppermute(own, "core", SWAP)
    x_parts = gather_rows(block)

    piece_2, piece_3 = pieces(where, own, other)

    def spread(piece):
        low, high = halves(piece)
        left = lax.ppermute(low, "dp", ring(8, 1))
        right = lax.ppermute(high, "dp", ring(8, 7))
        found = (piece, left, right)
        return found + tuple(lax.ppermute(p, "core", SWAP) for p in found)

    far_2 = lax.ppermute(piece_2, "yh", [(1, 0)])
    weights = [(own, other), (own, other), None, None]

    saved = []
    qkv, x = first(where, x_parts, weights[0])
    far_3 = lax.ppermute(after(piece_3, qkv), "yh", [(1, 0)])
    grad_parts = gather_rows(after(cot, qkv))
    for layer in range(4):
        kv = lax.ppermute(qkv[:, QW:], "core", SWAP)
        near = near_attention(qkv) if layer else ()
        if layer == 3:
            att, tot, grad = last(where, qkv, kv, near, grad_parts)
            saved.append((x, qkv, kv, att, tot))
            continue
        att, tot, out, *more = attend(layer, where, qkv, kv, x, near, weights[layer])
        saved.append((x, qkv, kv, att, tot))
        x = out
        if layer == 0:
            weights[2] = spread(after(far_2, x))
        if layer == 1:
            weights[3] = spread(after(far_3, x))
        qkv = more[0] if more else later(layer + 1, where, x, weights[layer + 1])

    terms = far_terms = None
    for layer in (3, 2, 1, 0):
        x, qkv, kv, att, tot = saved[layer]
        part, far_part, scaled, corr, turned = far_scores(
            layer, where, grad, qkv, kv, att, tot, weights[layer]
        )
        got = lax.ppermute(far_part, "core", SWAP)
        gq, own_part = own_scores(qkv, part, scaled, corr, turned)
        prev = terms if layer % 2 == 0 else None
        grad, terms, *give = input_grads(
            layer, where, own_part, got, gq, x, grad, att, pick, weights[layer], prev
        )
        if layer % 2 == 0:
            met = lax.ppermute(give[0], "core", SWAP)
        if layer == 2:
            early = join(where, terms, met)
            far_terms = lax.ppermute(early, "yh", [(0, 1)])

    kept, to_other = own_block(where, grad)
    both = jnp.where(core == yl, kept, lax.ppermute(to_other, "core", SWAP))
    d_far = lax.ppermute(both[:, 384:], "yh", [(0, 1)])
    d_acts = jnp.where(yh == 0, both[:, :384], d_far)

    payload = join(where, terms, met, far_terms).reshape(8, 24, TERMS)
    sums = jnp.sum(lax.all_to_all(payload, "dp", 0, 0).astype(F32), axis=0)
    return (
        d_acts[None],
        sums[:, ALL].reshape(1, 24),
        sums[None, :, :QW],
        sums[None, :, QW : 2 * QW],
        sums[None, :, 2 * QW : QKV],
        sums[None, :, QKV:ALL],
    )


def solution(mesh):
    fine = Mesh(mesh.devices.reshape(8, 2, 2, 2, 4), AXES)
    section = ("yh", "core")
    seq = ("yl", "x")
    rows = ("dp", "yl", "x")
    return jax.shard_map(
        program,
        mesh=fine,
        in_specs=(
            P("dp", seq, None),
            P("dp", seq, None),
            P(section, None),
            P(section, None, None),
            P(section, None, None),
            P(section, None, None),
            P(section, None, None),
        ),
        out_specs=(
            P("dp", seq, section),
            P(section, rows),
            P(section, rows, None),
            P(section, rows, None),
            P(section, rows, None),
            P(section, rows, None),
        ),
        check_vma=False,
    )
```
